128 devices in a mesh: row: 16 (over y, z), col: 8 (over x, core).
Axes of the slice: x: 4, y: 4, z: 4, core: 2. Of those that a mesh axis runs over, the one named last changes fastest.
Arguments:
- inputs: bfloat16 [768, 8192], P('row', 'col'), may hold values from -16 to 16
- norm_gain: float32 [8192], P('col'), may hold values from 0.25 to 4
- w_gate: bfloat16 [8192, 28672], P('col', 'row'), may hold values from -0.09375 to 0.09375
- w_up: bfloat16 [8192, 28672], P('col', 'row'), may hold values from -0.09375 to 0.09375
- w_down: bfloat16 [28672, 8192], P('row', 'col'), may hold values from -0.050111483 to 0.050111483
- mask_gate: int32 [128, 448], P('col', 'row'), may hold values 0 or 1
- mask_up: int32 [128, 448], P('col', 'row'), may hold values 0 or 1
- mask_down: int32 [448, 128], P('row', 'col'), may hold values 0 or 1
- grad_out: bfloat16 [768, 8192], P('row', 'col'), may hold values from -5 to 5
Outputs:
- output: bfloat16 [768, 8192], P('row', 'col')
- grad_inputs: bfloat16 [768, 8192], P('row', 'col')
- grad_gain: float32 [8192], P('col')
- grad_w_gate: bfloat16 [8192, 28672], P('col', 'row')
- grad_w_up: bfloat16 [8192, 28672], P('col', 'row')
- grad_w_down: bfloat16 [28672, 8192], P('row', 'col')
The draws below stay inside these ranges and needn't reach their ends.
All inputs are finite; a program needn't handle non-finite values. No bound on the sum of `mask_gate` or of `mask_up` or of `mask_down` on one device may be relied on, other than what follows from the above.
Results may differ from the reference program's by a relative error of at most 0.02.
Values may be sent and summed in bfloat16 or wider, within the bound.
A program may use at most 128 MiB of HBM per device.

```python
import jax
import jax.numpy as jnp
from jax import lax

D = 8192
FF = 28672
BLOCK = 64
TOKENS = 768
N_ROW = 16
N_COL = 8


def feature_ramp(low_end, high_end):
    position = jnp.arange(D, dtype=jnp.float32) / max(D - 1, 1)
    return low_end * jnp.exp(position * jnp.log(high_end / low_end))


def unit_noise(noise_key, shape):
    return jax.random.truncated_normal(noise_key, -4.0, 4.0, shape, jnp.float32)


def feature_signs(key):
    picked = jax.random.bernoulli(jax.random.fold_in(key, 21), 0.5, (D,))
    return jnp.where(picked, 1.0, -1.0).astype(jnp.float32)


def shared_gate_noise(key):
    return unit_noise(jax.random.fold_in(key, 11), (D, FF))


def draw_inputs(key, part):
    first_key, second_key = jax.random.split(key)
    ramp = feature_ramp(1.0, 3.0) * jax.random.uniform(second_key, (D,), jnp.float32, 0.8, 1.25)
    values = jax.random.truncated_normal(first_key, -4.0, 4.0, (TOKENS, D), jnp.float32)
    return (values * ramp).astype(jnp.bfloat16)


def draw_norm_gain(key, part):
    ramp = feature_ramp(0.5, 2.0) * jax.random.uniform(key, (D,), jnp.float32, 0.8, 1.25)
    return ramp.astype(jnp.float32)


def draw_w_gate(key, part):
    spread = float(D // 2) ** (-0.5)
    return (shared_gate_noise(key) * spread).astype(jnp.bfloat16)


def draw_w_up(key, part):
    spread = float(D // 2) ** (-0.5)
    linked = 0.9
    own_noise = unit_noise(jax.random.fold_in(key, 12), (D, FF))
    mixed = linked * shared_gate_noise(key) + (1.0 - linked * linked) ** 0.5 * own_noise
    return (mixed * spread).astype(jnp.bfloat16)


def draw_w_down(key, part):
    spread = float(FF // 2) ** (-0.5)
    offset = 4.0 / FF
    noise = unit_noise(jax.random.fold_in(key, 13), (FF, D))
    return (noise * spread + offset * feature_signs(key)[None, :]).astype(jnp.bfloat16)


def draw_grad_out(key, part):
    amplitude = jax.random.uniform(jax.random.fold_in(key, 31), (TOKENS, 1), jnp.float32, 0.3, 0.6)
    noise = unit_noise(jax.random.fold_in(key, 14), (TOKENS, D))
    return (noise + amplitude * feature_signs(key)[None, :]).astype(jnp.bfloat16)


def touch_ends(entries, rng, low, largest):
    place = [jax.random.randint(jax.random.fold_in(rng, axis), (), 0, length) for axis, length in enumerate(entries.shape)]
    longest = entries.shape.index(max(entries.shape))
    beside = place[:longest] + [(place[longest] + 1) % entries.shape[longest]] + place[longest + 1:]
    return entries.at[tuple(place)].set(low).at[tuple(beside)].set(largest)


def setup_inputs(seed: int = 0) -> dict:
    keys = jax.random.split(jax.random.key(seed), 10)
    inputs = draw_inputs(jax.random.fold_in(keys[9], 71), 0)
    norm_gain = draw_norm_gain(jax.random.fold_in(keys[9], 71), 0)
    w_gate = draw_w_gate(jax.random.fold_in(keys[9], 71), 0)
    w_up = draw_w_up(jax.random.fold_in(keys[9], 71), 0)
    w_down = draw_w_down(jax.random.fold_in(keys[9], 71), 0)
    mask_gate = touch_ends((jax.random.randint(keys[5], (D // BLOCK, FF // BLOCK), 0, 2) < 1).astype(jnp.int32), jax.random.fold_in(keys[5], 1), 0, 1)
    mask_up = touch_ends((jax.random.randint(keys[6], (D // BLOCK, FF // BLOCK), 0, 2) < 1).astype(jnp.int32), jax.random.fold_in(keys[6], 1), 0, 1)
    mask_down = touch_ends((jax.random.randint(keys[7], (FF // BLOCK, D // BLOCK), 0, 2) < 1).astype(jnp.int32), jax.random.fold_in(keys[7], 1), 0, 1)
    grad_out = draw_grad_out(jax.random.fold_in(keys[9], 71), 0)
    return {"inputs": inputs, "norm_gain": norm_gain, "w_gate": w_gate, "w_up": w_up, "w_down": w_down, "mask_gate": mask_gate, "mask_up": mask_up, "mask_down": mask_down, "grad_out": grad_out}


epsilon = 1e-05

def expand_mask(weight, block_mask):
    mask_rows, mask_cols = block_mask.shape
    blocked = weight.reshape(mask_rows, BLOCK, mask_cols, BLOCK) * block_mask.astype(jnp.bfloat16)[:, None, :, None]
    return blocked.reshape(weight.shape)

def contract_rows(left, right):
    return lax.dot_general(left, right, (((0,), (0,)), ((), ())), preferred_element_type=jnp.float32)

def piecewise(pairs, pieces, left_axis, right_axis):
    width = pairs[0][0].shape[left_axis] // pieces
    total = None
    for index in range(pieces):
        term = None
        for left, right in pairs:
            left_piece = lax.slice_in_dim(left, index * width, (index + 1) * width, axis=left_axis)
            right_piece = lax.slice_in_dim(right, index * width, (index + 1) * width, axis=right_axis)
            product = lax.dot_general(left_piece, right_piece, (((left_axis,), (right_axis,)), ((), ())), preferred_element_type=jnp.float32)
            term = product if term is None else term + product
        rounded = lax.optimization_barrier(term.astype(jnp.bfloat16)).astype(jnp.float32)
        total = rounded if total is None else total + rounded
    return total

def reference(inputs, norm_gain, w_gate, w_up, w_down, mask_gate, mask_up, mask_down, grad_out):
    gate_eff = expand_mask(w_gate, mask_gate)
    up_eff = expand_mask(w_up, mask_up)
    down_eff = expand_mask(w_down, mask_down)
    inputs_wide = inputs.astype(jnp.float32)
    inv_rms = lax.rsqrt(lax.optimization_barrier(jnp.mean(inputs_wide * inputs_wide, axis=1, keepdims=True)) + epsilon)
    normed = inputs_wide * inv_rms
    hidden_in = (normed * norm_gain).astype(jnp.bfloat16)
    gate_value = piecewise([(hidden_in, gate_eff)], N_COL, 1, 0)
    up_value = piecewise([(hidden_in, up_eff)], N_COL, 1, 0)
    sigmoid_gate = jax.nn.sigmoid(gate_value)
    silu_gate = gate_value * sigmoid_gate
    hidden = (silu_gate * up_value).astype(jnp.bfloat16)
    output = (inputs_wide + piecewise([(hidden, down_eff)], N_ROW, 1, 0)).astype(jnp.bfloat16)
    d_hidden = piecewise([(grad_out, down_eff)], N_COL, 1, 1)
    grad_w_down = expand_mask(contract_rows(hidden, grad_out).astype(jnp.bfloat16), mask_down)
    d_up = (d_hidden * silu_gate).astype(jnp.bfloat16)
    d_gate = (d_hidden * up_value * sigmoid_gate * (1.0 + gate_value * (1.0 - sigmoid_gate))).astype(jnp.bfloat16)
    grad_w_gate = expand_mask(contract_rows(hidden_in, d_gate).astype(jnp.bfloat16), mask_gate)
    grad_w_up = expand_mask(contract_rows(hidden_in, d_up).astype(jnp.bfloat16), mask_up)
    d_norm_in = piecewise([(d_gate, gate_eff), (d_up, up_eff)], N_ROW, 1, 1)
    grad_gain = lax.optimization_barrier(jnp.sum(d_norm_in * normed, axis=0))
    d_normed = d_norm_in * norm_gain
    row_inner = lax.optimization_barrier(jnp.sum(d_normed * normed, axis=1, keepdims=True)) / D
    grad_inputs = (grad_out.astype(jnp.float32) + inv_rms * (d_normed - normed * row_inner)).astype(jnp.bfloat16)
    return (output, grad_inputs, grad_gain, grad_w_gate, grad_w_up, grad_w_down)
```

```python
import functools

import jax
import jax.numpy as jnp
from jax import lax
from jax.experimental import pallas as pl
from jax.experimental.pallas import tpu as pltpu
from jax.sharding import PartitionSpec as P

D = 8192
BLOCK = 64
EPSILON = 1e-05
MESH = pl.DeviceIdType.MESH
F32 = jnp.float32
BF16 = jnp.bfloat16

LOCAL = 48
CHUNKS = 3
SUB = 16
FEATS = 1024
UNITS = 1792
HALF = FEATS // 2
TILE = 256
COPIES = 320


def nt_dot(left, right):
    return lax.dot_general(left, right, (((1,), (1,)), ((), ())), preferred_element_type=F32)


def nn_dot(left, right):
    return lax.dot_general(left, right, (((1,), (0,)), ((), ())), preferred_element_type=F32)


def lane_fold(value):
    total = value[:, 0:128]
    for start in range(128, value.shape[1], 128):
        total = total + value[:, start : start + 128]
    return total


def layer(
    inputs, gain, w_gate, w_up, w_down, mask_gate, mask_up, mask_down, grad_out,
    output, grad_inputs, grad_gain, grad_w_gate, grad_w_up, grad_w_down,
    wg, wu, wd, eg, eu, ed, hid, cot, part, pair, fwd_a, fwd_b, from_l, from_r, act,
    row_part, row_in1, row_sum, row_in2, normed, inv_rms, d_norm,
    sq_own, sq_in, in_own, in_in, gn_own, gn_in, stage, turned,
    send_sem, recv_sem, load_sem, store_sem,
):
    row = lax.axis_index("row")
    col = lax.axis_index("col")
    y, z = row // 4, lax.rem(row, 4)
    x, core = col // 2, lax.rem(col, 2)

    def up(value, steps):
        return lax.rem(value + steps, 4)

    def at_x(steps, other=0):
        return (row, up(x, steps) * 2 + (1 - core if other else core))

    def at_y(steps):
        return (up(y, steps) * 4 + z, col)

    def at_z(steps):
        return (y * 4 + up(z, steps), col)

    partner = at_x(0, 1)
    started = []

    def send(src, dst, device):
        index = len(started)
        copy = pltpu.make_async_remote_copy(
            src_ref=src, dst_ref=dst, send_sem=send_sem.at[index], recv_sem=recv_sem.at[index],
            device_id=device, device_id_type=MESH,
        )
        copy.start()
        started.append(copy)
        return copy

    def arrive(copies):
        for copy in copies:
            copy.wait_recv()

    loads = [
        pltpu.make_async_copy(source, target, load_sem.at[index])
        for index, (source, target) in enumerate(((w_down, wd), (w_gate, wg), (w_up, wu)))
    ]
    for load in loads:
        load.start()

    barrier = pltpu.get_barrier_semaphore()
    neighbours = [partner]
    for steps in (1, 2, 3):
        neighbours += [at_x(steps), at_x(steps, 1), at_y(steps), at_z(steps)]
    for device in neighbours:
        pl.semaphore_signal(barrier, inc=1, device_id=device, device_id_type=MESH)

    for k in range(CHUNKS):
        cot[k, y, z] = grad_out[k * SUB : (k + 1) * SUB, :]
    wide = inputs[...].astype(F32)
    sq_own[...] = lane_fold(wide * wide)

    pl.semaphore_wait(barrier, len(neighbours))

    def all_col(own, into):
        copies = [send(own, into.at[0], partner)]
        for steps in (1, 2, 3):
            copies.append(send(own, into.at[2 * steps - 1], at_x(steps)))
            copies.append(send(own, into.at[2 * steps], at_x(steps, 1)))
        return copies

    def gather1(ref, k):
        copies = []
        for steps in (1, 2, 3):
            part_a = ref.at[k, y, z, :, pl.ds(0, HALF)]
            part_b = ref.at[k, y, z, :, pl.ds(HALF, HALF)]
            copies.append(send(part_a, part_a, at_z(steps)))
            copies.append(send(part_b, part_b, at_y(steps)))
        return copies

    def gather2(ref, k):
        copies = []
        for steps in (1, 2, 3):
            part_a = ref.at[k, y, :, :, pl.ds(0, HALF)]
            part_b = ref.at[k, :, z, :, pl.ds(HALF, HALF)]
            copies.append(send(part_a, part_a, at_y(steps)))
            copies.append(send(part_b, part_b, at_z(steps)))
        return copies

    squares = all_col(sq_own, sq_in)
    cot1 = [gather1(cot, k) for k in range(CHUNKS)]

    def widen(mask_ref, into):
        rows, blocks = mask_ref.shape
        width = blocks * BLOCK
        unit = lax.broadcasted_iota(jnp.int32, (blocks, width), 1)
        first = lax.broadcasted_iota(jnp.int32, (blocks, width), 0) * BLOCK
        spread = jnp.where((unit >= first) & (unit < first + BLOCK), 1.0, 0.0).astype(BF16)
        wide_mask = nn_dot(mask_ref[...].astype(F32).astype(BF16), spread)
        for r in range(rows):
            into[r] = jnp.broadcast_to(wide_mask[r : r + 1, :], (SUB, width)).astype(BF16)

    def mask_weights(ref, wide_mask, load):
        load.wait()

        def body(r, carry):
            kept = wide_mask[r]
            for piece in range(BLOCK // SUB):
                rows = pl.ds(pl.multiple_of(r * BLOCK + piece * SUB, SUB), SUB)
                ref[rows, :] = ref[rows, :] * kept
            return carry

        lax.fori_loop(0, wide_mask.shape[0], body, 0)

    widen(mask_down, ed)
    mask_weights(wd, ed, loads[0])

    arrive(squares)
    squares_all = sq_own[...]
    for index in range(7):
        squares_all = squares_all + sq_in[index]
    inv_rms[...] = jnp.broadcast_to(
        lax.rsqrt(jnp.sum(squares_all, axis=1, keepdims=True) / D + EPSILON), (LOCAL, 128)
    )
    scale = inv_rms[:, 0:1]
    normed[...] = inputs[...].astype(F32) * scale
    own_hidden_in = (normed[...] * gain[...]).astype(BF16)
    for k in range(CHUNKS):
        hid[k, y, z] = own_hidden_in[k * SUB : (k + 1) * SUB, :]
    hid1 = [gather1(hid, k) for k in range(CHUNKS)]

    arrive(cot1[0])
    cot2 = {0: gather2(cot, 0)}
    arrive(hid1[0])
    hid2 = {0: gather2(hid, 0)}
    for k in (1, 2):
        arrive(cot1[k])
        cot2[k] = gather2(cot, k)
        arrive(hid1[k])
        hid2[k] = gather2(hid, k)

    widen(mask_gate, eg)
    widen(mask_up, eu)
    mask_weights(wg, eg, loads[1])
    mask_weights(wu, eu, loads[2])

    def chunk_of(ref, k):
        return ref[k].reshape(CHUNKS and 4 * 4 * SUB, FEATS)

    def tiles(count, body):
        def step(n, carry):
            body(pl.multiple_of(n * TILE, TILE))
            return carry

        lax.fori_loop(0, count, step, 0)

    def pair_send(k, start, width):
        return [
            send(
                part.at[k, pl.ds(pl.multiple_of((1 - core) * 128, 128), 128), pl.ds(start, width)],
                pair.at[k, :, pl.ds(start, width)],
                partner,
            )
        ]

    def mm_down_back(k):
        arrive(cot2[k])

        def body(at):
            product = nt_dot(chunk_of(cot, k), wd[pl.ds(at, TILE), :])
            part[k, :, pl.ds(at, TILE)] = product.astype(BF16)

        tiles(UNITS // TILE, body)
        return pair_send(k, 0, UNITS)

    def mm_gate_up(k):
        arrive(hid2[k])

        def body(at):
            left = chunk_of(hid, k)
            part[k, :, pl.ds(UNITS + at, TILE)] = nn_dot(left, wg[:, pl.ds(at, TILE)]).astype(BF16)
            part[k, :, pl.ds(2 * UNITS + at, TILE)] = nn_dot(left, wu[:, pl.ds(at, TILE)]).astype(BF16)

        tiles(UNITS // TILE, body)
        return pair_send(k, UNITS, 2 * UNITS)

    def block_rows(which, offset, count):
        return pl.ds(pl.multiple_of(which * 32 + offset, SUB), count)

    def scatter1(k, job, copies):
        start, width = job
        cols = pl.ds(start, width)
        arrive(copies)
        mine = pl.multiple_of(core * 128, 128)
        def body(r, carry):
            rows = pl.ds(pl.multiple_of(r * SUB, SUB), SUB)
            own = part[k, pl.ds(pl.multiple_of(mine + r * SUB, SUB), SUB), cols].astype(F32)
            pair[k, rows, cols] = (own + pair[k, rows, cols].astype(F32)).astype(BF16)
            return carry
        lax.fori_loop(0, 8, body, 0)
        right, left = at_x(1), at_x(3)
        two = up(x, 2)
        return (
            send(pair.at[k, block_rows(two, 0, SUB), cols], fwd_a.at[k, :, cols], right),
            send(pair.at[k, block_rows(two, SUB, SUB), cols], fwd_b.at[k, :, cols], left),
            send(pair.at[k, block_rows(up(x, 1), SUB, SUB), cols], from_l.at[k, pl.ds(SUB, SUB), cols], right),
            send(pair.at[k, block_rows(up(x, 3), 0, SUB), cols], from_r.at[k, pl.ds(0, SUB), cols], left),
        )

    def scatter2(k, job, copies):
        start, width = job
        cols = pl.ds(start, width)
        right, left = at_x(1), at_x(3)
        arrive(copies[0:1])
        own = pair[k, block_rows(up(x, 1), 0, SUB), cols].astype(F32)
        fwd_a[k, :, cols] = (own + fwd_a[k, :, cols].astype(F32)).astype(BF16)
        first = send(fwd_a.at[k, :, cols], from_l.at[k, pl.ds(0, SUB), cols], right)
        arrive(copies[1:2])
        own = pair[k, block_rows(up(x, 3), SUB, SUB), cols].astype(F32)
        fwd_b[k, :, cols] = (own + fwd_b[k, :, cols].astype(F32)).astype(BF16)
        second = send(fwd_b.at[k, :, cols], from_r.at[k, pl.ds(SUB, SUB), cols], left)
        return (copies[2], copies[3], first, second)

    down_job, gate_up_job = (0, UNITS), (UNITS, 2 * UNITS)
    owner = core * 4 + x

    def activate(k, copies):
        arrive(copies)
        def total(start):
            cols = pl.ds(start, 256)
            return (
                pair[k, block_rows(x, 0, 32), cols].astype(F32)
                + from_l[k, :, cols].astype(F32)
                + from_r[k, :, cols].astype(F32)
            )

        def body(at):
            d_hidden = total(at)
            gate_value = total(UNITS + at)
            up_value = total(2 * UNITS + at)
            sigma = jax.nn.sigmoid(gate_value)
            silu = gate_value * sigma
            rows = block_rows(owner, 0, 32)
            act[k, rows, pl.ds(at, 256)] = (silu * up_value).astype(BF16)
            act[k, rows, pl.ds(UNITS + at, 256)] = (
                d_hidden * up_value * sigma * (1.0 + gate_value * (1.0 - sigma))
            ).astype(BF16)
            act[k, rows, pl.ds(2 * UNITS + at, 256)] = (d_hidden * silu).astype(BF16)

        tiles(UNITS // 256, body)
        block = act.at[k, block_rows(owner, 0, 32), :]
        return (
            send(block, block, at_x(1)),
            send(block, block, at_x(3)),
            send(block, block, partner),
        )

    def spread2(k, copies):
        from_left, from_right = core * 4 + up(x, 3), core * 4 + up(x, 1)
        arrive(copies[0:1])
        half = act.at[k, block_rows(from_left, 0, SUB), :]
        block = act.at[k, block_rows(from_left, 0, 32), :]
        first = send(half, half, at_x(1))
        first_pair = send(block, block, partner)
        arrive(copies[1:2])
        half = act.at[k, block_rows(from_right, SUB, SUB), :]
        block = act.at[k, block_rows(from_right, 0, 32), :]
        second = send(half, half, at_x(3))
        second_pair = send(block, block, partner)
        return (first, second), (copies[2], first_pair, second_pair)

    def spread3(k, halves, pairs):
        arrive(halves)
        block = act.at[k, block_rows(core * 4 + up(x, 2), 0, 32), :]
        return pairs + (send(block, block, partner),)

    def row_scatter1(which, k):
        copies = []
        for steps in (1, 2, 3):
            copies.append(send(
                row_part.at[which, k, up(y, steps), :, :, pl.ds(0, HALF)],
                row_in1.at[which, k, steps - 1, :, :, pl.ds(0, HALF)], at_y(steps)))
            copies.append(send(
                row_part.at[which, k, :, up(z, steps), :, pl.ds(HALF, HALF)],
                row_in1.at[which, k, steps - 1, :, :, pl.ds(HALF, HALF)], at_z(steps)))
        return copies

    def row_scatter2(which, k, copies):
        arrive(copies)
        sum_a = row_part[which, k, y, :, :, 0:HALF].astype(F32)
        sum_b = row_part[which, k, :, z, :, HALF:FEATS].astype(F32)
        for index in range(3):
            sum_a = sum_a + row_in1[which, k, index, :, :, 0:HALF].astype(F32)
            sum_b = sum_b + row_in1[which, k, index, :, :, HALF:FEATS].astype(F32)
        row_sum[which, k, :, :, 0:HALF] = sum_a.astype(BF16)
        row_sum[which, k, :, :, HALF:FEATS] = sum_b.astype(BF16)
        after = []
        for steps in (1, 2, 3):
            after.append(send(
                row_sum.at[which, k, up(z, steps), :, pl.ds(0, HALF)],
                row_in2.at[which, k, steps - 1, :, pl.ds(0, HALF)], at_z(steps)))
            after.append(send(
                row_sum.at[which, k, up(y, steps), :, pl.ds(HALF, HALF)],
                row_in2.at[which, k, steps - 1, :, pl.ds(HALF, HALF)], at_y(steps)))
        return after

    def row_total(which, k, copies, start):
        other = z if start == 0 else y
        total = row_sum[which, k, other, :, start : start + HALF].astype(F32)
        for index in range(3):
            total = total + row_in2[which, k, index, :, start : start + HALF].astype(F32)
        return total

    def mm_out(k, pairs):
        arrive(pairs)

        def body(at):
            product = nn_dot(act[k, :, 0:UNITS], wd[:, pl.ds(at, TILE)]).astype(BF16)
            row_part[0, k, :, :, :, pl.ds(at, TILE)] = product.reshape(4, 4, SUB, TILE)

        tiles(FEATS // TILE, body)
        return row_scatter1(0, k)

    def mm_in_back(k):
        def body(at):
            product = nt_dot(act[k, :, UNITS : 2 * UNITS], wg[pl.ds(at, TILE), :]) + nt_dot(
                act[k, :, 2 * UNITS : 3 * UNITS], wu[pl.ds(at, TILE), :]
            )
            row_part[1, k, :, :, :, pl.ds(at, TILE)] = product.astype(BF16).reshape(4, 4, SUB, TILE)

        tiles(FEATS // TILE, body)
        return row_scatter1(1, k)

    def finish_out(k, copies):
        arrive(copies)
        rows = slice(k * SUB, (k + 1) * SUB)
        for start in (0, HALF):
            total = row_total(0, k, copies, start)
            output[rows, start : start + HALF] = (
                inputs[rows, start : start + HALF].astype(F32) + total
            ).astype(BF16)

    def finish_in(k, copies):
        arrive(copies)
        rows = slice(k * SUB, (k + 1) * SUB)
        for start in (0, HALF):
            d_norm[rows, start : start + HALF] = row_total(1, k, copies, start)

    stores = []

    def weight_grad(left_of, right_of, units, width, wide_mask, target, slot):
        def rows_body(m, carry):
            at = pl.multiple_of(m * TILE, TILE)
            use = lax.rem(m, 2)
            turned[...] = left_of(at).T
            @pl.when(m >= 2)
            def _():
                pltpu.make_async_copy(
                    stage.at[use, :, pl.ds(0, width)], target.at[pl.ds(at, TILE), :], store_sem.at[slot + use]
                ).wait()

            def cols_body(n, inner):
                to = pl.multiple_of(n * TILE, TILE)
                product = nn_dot(turned[...], right_of(to)).astype(BF16)
                kept = wide_mask[pl.ds(m * 4, 4), :, pl.ds(to, TILE)]
                product = product.reshape(4, 4, SUB, TILE) * kept.reshape(4, 1, SUB, TILE)
                stage[use, :, pl.ds(to, TILE)] = product.reshape(TILE, TILE)
                return inner

            lax.fori_loop(0, width // TILE, cols_body, 0)
            pltpu.make_async_copy(
                stage.at[use, :, pl.ds(0, width)], target.at[pl.ds(at, TILE), :], store_sem.at[slot + use]
            ).start()
            return carry

        lax.fori_loop(0, units // TILE, rows_body, 0)
        for use in range(2):
            pltpu.make_async_copy(
                stage.at[use, :, pl.ds(0, width)], target.at[pl.ds(0, TILE), :], store_sem.at[slot + use]
            ).wait()

    tokens = CHUNKS * 256

    def act_cols(start):
        def get(at):
            return act[:, :, pl.ds(pl.multiple_of(start + at, TILE), TILE)].reshape(tokens, TILE)

        return get

    def token_cols(ref):
        def get(at):
            return ref[:, :, :, :, pl.ds(at, TILE)].reshape(tokens, TILE)

        return get

    pd0 = mm_down_back(0)
    pg0 = mm_gate_up(0)
    sd0 = scatter1(0, down_job, pd0)
    pd1 = mm_down_back(1)
    sg0 = scatter1(0, gate_up_job, pg0)
    td0 = scatter2(0, down_job, sd0)
    pg1 = mm_gate_up(1)
    sd1 = scatter1(1, down_job, pd1)
    tg0 = scatter2(0, gate_up_job, sg0)
    sg1 = scatter1(1, gate_up_job, pg1)
    td1 = scatter2(1, down_job, sd1)
    pd2 = mm_down_back(2)
    pg2 = mm_gate_up(2)
    a0 = activate(0, td0 + tg0)
    tg1 = scatter2(1, gate_up_job, sg1)
    sd2 = scatter1(2, down_job, pd2)
    h0, q0 = spread2(0, a0)
    sg2 = scatter1(2, gate_up_job, pg2)
    a1 = activate(1, td1 + tg1)
    td2 = scatter2(2, down_job, sd2)
    r0 = spread3(0, h0, q0)
    tg2 = scatter2(2, gate_up_job, sg2)
    h1, q1 = spread2(1, a1)
    o0 = mm_out(0, r0)
    n0 = mm_in_back(0)
    a2 = activate(2, td2 + tg2)
    r1 = spread3(1, h1, q1)
    h2, q2 = spread2(2, a2)
    o0 = row_scatter2(0, 0, o0)
    n0 = row_scatter2(1, 0, n0)
    o1 = mm_out(1, r1)
    n1 = mm_in_back(1)
    r2 = spread3(2, h2, q2)
    finish_out(0, o0)
    finish_in(0, n0)
    o1 = row_scatter2(0, 1, o1)
    n1 = row_scatter2(1, 1, n1)
    o2 = mm_out(2, r2)
    n2 = mm_in_back(2)
    weight_grad(act_cols(0), token_cols(cot), UNITS, FEATS, ed, grad_w_down, 0)
    o2 = row_scatter2(0, 2, o2)
    n2 = row_scatter2(1, 2, n2)
    finish_out(1, o1)
    finish_in(1, n1)
    weight_grad(token_cols(hid), act_cols(UNITS), FEATS, UNITS, eg, grad_w_gate, 0)
    finish_out(2, o2)
    finish_in(2, n2)

    moved = d_norm[...] * normed[...]
    in_own[...] = lane_fold(moved * gain[...])
    inner = all_col(in_own, in_in)
    folded = moved[0:8]
    for start in range(8, LOCAL, 8):
        folded = folded + moved[start : start + 8]
    gn_own[0] = folded
    gains = [send(gn_own.at[0], gn_in.at[steps - 1], at_z(steps)) for steps in (1, 2, 3)]
    arrive(gains)
    gn_own[1] = gn_own[0] + gn_in[0] + gn_in[1] + gn_in[2]
    gains = [send(gn_own.at[1], gn_in.at[steps + 2], at_y(steps)) for steps in (1, 2, 3)]
    weight_grad(token_cols(hid), act_cols(2 * UNITS), FEATS, UNITS, eu, grad_w_up, 0)
    arrive(gains)
    grad_gain[...] = jnp.sum(gn_own[1] + gn_in[3] + gn_in[4] + gn_in[5], axis=0, keepdims=True)
    arrive(inner)
    inner_all = in_own[...]
    for index in range(7):
        inner_all = inner_all + in_in[index]
    row_inner = jnp.sum(inner_all, axis=1, keepdims=True) / D
    grad_inputs[...] = (
        grad_out[...].astype(F32)
        + inv_rms[:, 0:1] * (d_norm[...] * gain[...] - normed[...] * row_inner)
    ).astype(BF16)

    for copy in started:
        copy.wait_send()


def shards(inputs, norm_gain, w_gate, w_up, w_down, mask_gate, mask_up, mask_down, grad_out):
    vmem = pl.BlockSpec(memory_space=pltpu.VMEM)
    anywhere = pl.BlockSpec(memory_space=pl.ANY)
    wide = 3 * UNITS
    shape = jax.ShapeDtypeStruct
    output, grad_inputs, grad_gain, grad_w_gate, grad_w_up, grad_w_down = pl.pallas_call(
        layer,
        out_shape=(
            shape((LOCAL, FEATS), BF16),
            shape((LOCAL, FEATS), BF16),
            shape((1, FEATS), F32),
            shape((FEATS, UNITS), BF16),
            shape((FEATS, UNITS), BF16),
            shape((UNITS, FEATS), BF16),
        ),
        in_specs=[vmem, vmem, anywhere, anywhere, anywhere, vmem, vmem, vmem, vmem],
        out_specs=(vmem, vmem, vmem, anywhere, anywhere, anywhere),
        scratch_shapes=[
            pltpu.VMEM((FEATS, UNITS), BF16),
            pltpu.VMEM((FEATS, UNITS), BF16),
            pltpu.VMEM((UNITS, FEATS), BF16),
            pltpu.VMEM((FEATS // BLOCK, SUB, UNITS), BF16),
            pltpu.VMEM((FEATS // BLOCK, SUB, UNITS), BF16),
            pltpu.VMEM((UNITS // BLOCK, SUB, FEATS), BF16),
            pltpu.VMEM((CHUNKS, 4, 4, SUB, FEATS), BF16),
            pltpu.VMEM((CHUNKS, 4, 4, SUB, FEATS), BF16),
            pltpu.VMEM((CHUNKS, 256, wide), BF16),
            pltpu.VMEM((CHUNKS, 128, wide), BF16),
            pltpu.VMEM((CHUNKS, SUB, wide), BF16),
            pltpu.VMEM((CHUNKS, SUB, wide), BF16),
            pltpu.VMEM((CHUNKS, 32, wide), BF16),
            pltpu.VMEM((CHUNKS, 32, wide), BF16),
            pltpu.VMEM((CHUNKS, 256, wide), BF16),
            pltpu.VMEM((2, CHUNKS, 4, 4, SUB, FEATS), BF16),
            pltpu.VMEM((2, CHUNKS, 3, 4, SUB, FEATS), BF16),
            pltpu.VMEM((2, CHUNKS, 4, SUB, FEATS), BF16),
            pltpu.VMEM((2, CHUNKS, 3, SUB, FEATS), BF16),
            pltpu.VMEM((LOCAL, FEATS), F32),
            pltpu.VMEM((LOCAL, 128), F32),
            pltpu.VMEM((LOCAL, FEATS), F32),
            pltpu.VMEM((LOCAL, 128), F32),
            pltpu.VMEM((7, LOCAL, 128), F32),
            pltpu.VMEM((LOCAL, 128), F32),
            pltpu.VMEM((7, LOCAL, 128), F32),
            pltpu.VMEM((2, 8, FEATS), F32),
            pltpu.VMEM((6, 8, FEATS), F32),
            pltpu.VMEM((2, TILE, UNITS), BF16),
            pltpu.VMEM((TILE, CHUNKS * 256), BF16),
            pltpu.SemaphoreType.DMA((COPIES,)),
            pltpu.SemaphoreType.DMA((COPIES,)),
            pltpu.SemaphoreType.DMA((3,)),
            pltpu.SemaphoreType.DMA((2,)),
        ],
        compiler_params=pltpu.CompilerParams(
            collective_id=0, has_side_effects=True, vmem_limit_bytes=60 << 20
        ),
        name="layer",
    )(
        inputs, norm_gain.reshape(1, FEATS), w_gate, w_up, w_down,
        mask_gate, mask_up, mask_down, grad_out,
    )
    return output, grad_inputs, grad_gain.reshape(FEATS), grad_w_gate, grad_w_up, grad_w_down


def solution(mesh):
    in_specs = (
        P("row", "col"),
        P("col"),
        P("col", "row"),
        P("col", "row"),
        P("row", "col"),
        P("col", "row"),
        P("col", "row"),
        P("row", "col"),
        P("row", "col"),
    )
    out_specs = (
        P("row", "col"),
        P("row", "col"),
        P("col"),
        P("col", "row"),
        P("col", "row"),
        P("row", "col"),
    )
    return jax.shard_map(shards, mesh=mesh, in_specs=in_specs, out_specs=out_specs, check_vma=False)
```

```python
import functools

import jax
import jax.numpy as jnp
from jax import lax
from jax.experimental import pallas as pl
from jax.experimental.pallas import tpu as pltpu
from jax.sharding import PartitionSpec as P

D = 8192
BLOCK = 64
EPSILON = 1e-05
MESH = pl.DeviceIdType.MESH
F32 = jnp.float32
BF16 = jnp.bfloat16

LOCAL = 48
CHUNKS = 3
SUB = 16
FEATS = 1024
UNITS = 1792
HALF = FEATS // 2
TILE = 256
COPIES = 320


def nt_dot(left, right):
    return lax.dot_general(left, right, (((1,), (1,)), ((), ())), preferred_element_type=F32)


def nn_dot(left, right):
    return lax.dot_general(left, right, (((1,), (0,)), ((), ())), preferred_element_type=F32)


def tn_dot(left, right):
    return lax.dot_general(left, right, (((0,), (0,)), ((), ())), preferred_element_type=F32)


def masked(product, wide_mask):
    rows, width = product.shape
    blocks = product.astype(BF16).reshape(rows // BLOCK, BLOCK // SUB, SUB, width)
    return (blocks * wide_mask.reshape(rows // BLOCK, 1, SUB, width)).reshape(rows, width)


def lane_fold(value):
    total = value[:, 0:128]
    for start in range(128, value.shape[1], 128):
        total = total + value[:, start : start + 128]
    return total


def widen(mask, into):
    rows, blocks = mask.shape
    width = blocks * BLOCK
    unit = lax.broadcasted_iota(jnp.int32, (blocks, width), 1)
    first = lax.broadcasted_iota(jnp.int32, (blocks, width), 0) * BLOCK
    spread = jnp.where((unit >= first) & (unit < first + BLOCK), 1.0, 0.0).astype(BF16)
    wide_mask = nn_dot(mask.astype(F32).astype(BF16), spread)
    for r in range(rows):
        into[r] = jnp.broadcast_to(wide_mask[r : r + 1, :], (SUB, width)).astype(BF16)


def layer(
    inputs, gain, w_gate, w_up, w_down, mask_gate, mask_up, mask_down, grad_out,
    output, grad_inputs, grad_gain, grad_w_gate, grad_w_down, d_up_all, hid_all,
    wg, wu, wd, eg, eu, ed, hid, cot, part, pair, fwd_a, fwd_b, from_l, from_r, act,
    row_part, row_in1, row_sum, row_in2, normed, inv_rms, d_norm,
    sq_own, sq_in, in_own, in_in, gn_own, gn_in, stage_d, stage_u,
    send_sem, recv_sem, load_sem, store_sem, keep_sem,
):
    row = lax.axis_index("row")
    col = lax.axis_index("col")
    y, z = row // 4, lax.rem(row, 4)
    x, core = col // 2, lax.rem(col, 2)

    def up(value, steps):
        return lax.rem(value + steps, 4)

    def at_x(steps, other=0):
        return (row, up(x, steps) * 2 + (1 - core if other else core))

    def at_y(steps):
        return (up(y, steps) * 4 + z, col)

    def at_z(steps):
        return (y * 4 + up(z, steps), col)

    partner = at_x(0, 1)
    started = []

    def send(src, dst, device):
        index = len(started)
        copy = pltpu.make_async_remote_copy(
            src_ref=src, dst_ref=dst, send_sem=send_sem.at[index], recv_sem=recv_sem.at[index],
            device_id=device, device_id_type=MESH,
        )
        copy.start()
        started.append(copy)
        return copy

    kept = []

    def keep(source, target):
        copy = pltpu.make_async_copy(source, target, keep_sem.at[len(kept)])
        copy.start()
        kept.append(copy)

    def arrive(copies):
        for copy in copies:
            copy.wait_recv()

    loads = [
        pltpu.make_async_copy(source, target, load_sem.at[index])
        for index, (source, target) in enumerate(((w_down, wd), (w_gate, wg), (w_up, wu)))
    ]
    for load in loads:
        load.start()

    barrier = pltpu.get_barrier_semaphore()
    row_peers = [
        (up(y, steps // 4) * 4 + up(z, steps % 4), col) for steps in range(1, 16)
    ]
    neighbours = [partner] + row_peers
    for steps in (1, 2, 3):
        neighbours += [at_x(steps), at_x(steps, 1)]
    for device in neighbours:
        pl.semaphore_signal(barrier, inc=1, device_id=device, device_id_type=MESH)

    for k in range(CHUNKS):
        cot[k, y, z] = grad_out[k * SUB : (k + 1) * SUB, :]
    wide = inputs[...].astype(F32)
    sq_own[...] = lane_fold(wide * wide)

    pl.semaphore_wait(barrier, len(neighbours))

    def all_col(own, into):
        copies = [send(own, into.at[0], partner)]
        for steps in (1, 2, 3):
            copies.append(send(own, into.at[2 * steps - 1], at_x(steps)))
            copies.append(send(own, into.at[2 * steps], at_x(steps, 1)))
        return copies

    def gather1(ref, k):
        copies = []
        for steps in (1, 2, 3):
            part_a = ref.at[k, y, z, :, pl.ds(0, HALF)]
            part_b = ref.at[k, y, z, :, pl.ds(HALF, HALF)]
            copies.append(send(part_a, part_a, at_z(steps)))
            copies.append(send(part_b, part_b, at_y(steps)))
        return copies

    def gather2(ref, k):
        copies = []
        for steps in (1, 2, 3):
            part_a = ref.at[k, y, :, :, pl.ds(0, HALF)]
            part_b = ref.at[k, :, z, :, pl.ds(HALF, HALF)]
            copies.append(send(part_a, part_a, at_y(steps)))
            copies.append(send(part_b, part_b, at_z(steps)))
        return copies

    cot1 = [gather1(cot, 0)]
    squares = all_col(sq_own, sq_in)

    def mask_weights(ref, wide_mask, load):
        load.wait()

        def body(r, carry):
            kept = wide_mask[r]
            for piece in range(BLOCK // SUB):
                rows = pl.ds(pl.multiple_of(r * BLOCK + piece * SUB, SUB), SUB)
                ref[rows, :] = ref[rows, :] * kept
            return carry

        lax.fori_loop(0, wide_mask.shape[0], body, 0)

    widen(mask_down[...].astype(F32).T, ed)
    mask_weights(wd, ed, loads[0])
    arrive(cot1[0])
    cot2 = [gather2(cot, 0)]

    arrive(squares)
    squares_all = sq_own[...]
    for index in range(7):
        squares_all = squares_all + sq_in[index]
    inv_rms[...] = jnp.broadcast_to(
        lax.rsqrt(jnp.sum(squares_all, axis=1, keepdims=True) / D + EPSILON), (LOCAL, 128)
    )
    normed[...] = inputs[...].astype(F32) * inv_rms[:, 0:1]
    own_hidden_in = (normed[...] * gain[...]).astype(BF16)
    for k in range(CHUNKS):
        hid[k, y, z] = own_hidden_in[k * SUB : (k + 1) * SUB, :]
    hid1 = [gather1(hid, 0)]
    widen(mask_gate[...], eg)
    mask_weights(wg, eg, loads[1])
    arrive(hid1[0])
    hid2 = [gather2(hid, 0)]
    for k in (1, 2):
        cot1.append(gather1(cot, k))
        hid1.append(gather1(hid, k))
    widen(mask_up[...], eu)
    mask_weights(wu, eu, loads[2])

    def chunk_of(ref, k):
        return ref[k].reshape(4 * 4 * SUB, FEATS)

    def tiles(count, body):
        def step(n, carry):
            body(pl.multiple_of(n * TILE, TILE))
            return carry

        lax.fori_loop(0, count, step, 0)

    def pair_send(k, start, width):
        return [
            send(
                part.at[k, pl.ds(pl.multiple_of((1 - core) * 128, 128), 128), pl.ds(start, width)],
                pair.at[k, :, pl.ds(start, width)],
                partner,
            )
        ]

    def mm_down_back(k):
        arrive(cot2[k])
        copies = []
        for start in (0, UNITS // 2):
            rows = slice(start, start + UNITS // 2)
            part[k, :, rows] = nt_dot(chunk_of(cot, k), wd[rows, :]).astype(BF16)
            copies += pair_send(k, start, UNITS // 2)
        return copies

    def mm_gate(k):
        arrive(hid2[k])
        part[k, :, UNITS : 2 * UNITS] = nn_dot(chunk_of(hid, k), wg[...]).astype(BF16)
        return pair_send(k, UNITS, UNITS)

    def mm_up(k):
        part[k, :, 2 * UNITS : 3 * UNITS] = nn_dot(chunk_of(hid, k), wu[...]).astype(BF16)
        return pair_send(k, 2 * UNITS, UNITS)

    def block_rows(which, offset, count):
        return pl.ds(pl.multiple_of(which * 32 + offset, SUB), count)

    def scatter1(k, job, copies):
        start, width = job
        cols = pl.ds(start, width)
        arrive(copies)
        mine = pl.multiple_of(core * 128, 128)
        def body(r, carry):
            rows = pl.ds(pl.multiple_of(r * SUB, SUB), SUB)
            own = part[k, pl.ds(pl.multiple_of(mine + r * SUB, SUB), SUB), cols].astype(F32)
            pair[k, rows, cols] = (own + pair[k, rows, cols].astype(F32)).astype(BF16)
            return carry
        lax.fori_loop(0, 8, body, 0)
        right, left = at_x(1), at_x(3)
        two = up(x, 2)
        return (
            send(pair.at[k, block_rows(two, 0, SUB), cols], fwd_a.at[k, :, cols], right),
            send(pair.at[k, block_rows(two, SUB, SUB), cols], fwd_b.at[k, :, cols], left),
            send(pair.at[k, block_rows(up(x, 1), SUB, SUB), cols], from_l.at[k, pl.ds(SUB, SUB), cols], right),
            send(pair.at[k, block_rows(up(x, 3), 0, SUB), cols], from_r.at[k, pl.ds(0, SUB), cols], left),
        )

    def scatter2(k, job, copies):
        start, width = job
        cols = pl.ds(start, width)
        right, left = at_x(1), at_x(3)
        arrive(copies[0:1])
        own = pair[k, block_rows(up(x, 1), 0, SUB), cols].astype(F32)
        fwd_a[k, :, cols] = (own + fwd_a[k, :, cols].astype(F32)).astype(BF16)
        first = send(fwd_a.at[k, :, cols], from_l.at[k, pl.ds(0, SUB), cols], right)
        arrive(copies[1:2])
        own = pair[k, block_rows(up(x, 3), SUB, SUB), cols].astype(F32)
        fwd_b[k, :, cols] = (own + fwd_b[k, :, cols].astype(F32)).astype(BF16)
        second = send(fwd_b.at[k, :, cols], from_r.at[k, pl.ds(SUB, SUB), cols], left)
        return (copies[2], copies[3], first, second)

    down_job, gate_up_job = (0, UNITS), (UNITS, 2 * UNITS)
    gate_job, up_job = (UNITS, UNITS), (2 * UNITS, UNITS)
    owner = core * 4 + x

    def activate(k, copies):
        arrive(copies)
        def total(start):
            cols = pl.ds(start, 256)
            return (
                pair[k, block_rows(x, 0, 32), cols].astype(F32)
                + from_l[k, :, cols].astype(F32)
                + from_r[k, :, cols].astype(F32)
            )

        def body(at):
            d_hidden = total(at)
            gate_value = total(UNITS + at)
            up_value = total(2 * UNITS + at)
            sigma = jax.nn.sigmoid(gate_value)
            silu = gate_value * sigma
            rows = block_rows(owner, 0, 32)
            act[k, rows, pl.ds(at, 256)] = (silu * up_value).astype(BF16)
            act[k, rows, pl.ds(UNITS + at, 256)] = (
                d_hidden * up_value * sigma * (1.0 + gate_value * (1.0 - sigma))
            ).astype(BF16)
            act[k, rows, pl.ds(2 * UNITS + at, 256)] = (d_hidden * silu).astype(BF16)

        tiles(UNITS // 256, body)

    def spread1(k, job):
        block = act.at[k, block_rows(owner, 0, 32), pl.ds(*job)]
        return (
            send(block, block, at_x(1)),
            send(block, block, at_x(3)),
            send(block, block, partner),
        )

    def spread2(k, job, copies):
        cols = pl.ds(*job)
        from_left, from_right = core * 4 + up(x, 3), core * 4 + up(x, 1)
        arrive(copies[0:1])
        half = act.at[k, block_rows(from_left, 0, SUB), cols]
        block = act.at[k, block_rows(from_left, 0, 32), cols]
        first = send(half, half, at_x(1))
        first_pair = send(block, block, partner)
        arrive(copies[1:2])
        half = act.at[k, block_rows(from_right, SUB, SUB), cols]
        block = act.at[k, block_rows(from_right, 0, 32), cols]
        second = send(half, half, at_x(3))
        second_pair = send(block, block, partner)
        return (first, second), (copies[2], first_pair, second_pair)

    def spread3(k, job, halves, pairs):
        arrive(halves)
        block = act.at[k, block_rows(core * 4 + up(x, 2), 0, 32), pl.ds(*job)]
        return pairs + (send(block, block, partner),)

    halves = (slice(0, HALF), slice(HALF, FEATS))

    def row_scatter1(which, k, half):
        copies = []
        lanes = pl.ds(half * HALF, HALF)
        for steps in (1, 2, 3):
            into = row_in1.at[which, k, steps - 1, :, :, lanes]
            if half == 0:
                copies.append(send(row_part.at[which, k, up(y, steps), :, :, lanes], into, at_y(steps)))
            else:
                copies.append(send(row_part.at[which, k, :, up(z, steps), :, lanes], into, at_z(steps)))
        return copies

    def row_scatter2(which, k, half, copies):
        arrive(copies)
        lanes = halves[half]
        if half == 0:
            total = row_part[which, k, y, :, :, lanes].astype(F32)
        else:
            total = row_part[which, k, :, z, :, lanes].astype(F32)
        for index in range(3):
            total = total + row_in1[which, k, index, :, :, lanes].astype(F32)
        row_sum[which, k, :, :, lanes] = total.astype(BF16)
        after = []
        lanes = pl.ds(half * HALF, HALF)
        for steps in (1, 2, 3):
            into = row_in2.at[which, k, steps - 1, :, lanes]
            if half == 0:
                after.append(send(row_sum.at[which, k, up(z, steps), :, lanes], into, at_z(steps)))
            else:
                after.append(send(row_sum.at[which, k, up(y, steps), :, lanes], into, at_y(steps)))
        return after

    def row_scatters2(which, k, copies):
        return row_scatter2(which, k, 0, copies[0:3]) + row_scatter2(which, k, 1, copies[3:6])

    def row_total(which, k, half):
        lanes = halves[half]
        total = row_sum[which, k, y if half else z, :, lanes].astype(F32)
        for index in range(3):
            total = total + row_in2[which, k, index, :, lanes].astype(F32)
        return total

    def mm_out(k, pairs):
        arrive(pairs)
        product = nn_dot(act[k, :, 0:UNITS], wd[...]).astype(BF16)
        row_part[0, k] = product.reshape(4, 4, SUB, FEATS)
        return row_scatter1(0, k, 0) + row_scatter1(0, k, 1)

    def mm_in_back(k, pairs):
        arrive(pairs)
        keep(act.at[k, :, pl.ds(2 * UNITS, UNITS)], d_up_all.at[k])
        copies = []
        for half, lanes in enumerate(halves):
            product = nt_dot(act[k, :, UNITS : 2 * UNITS], wg[lanes, :]) + nt_dot(
                act[k, :, 2 * UNITS : 3 * UNITS], wu[lanes, :]
            )
            row_part[1, k, :, :, :, lanes] = product.astype(BF16).reshape(4, 4, SUB, HALF)
            copies += row_scatter1(1, k, half)
        return copies

    def finish_out(k, copies):
        arrive(copies)
        rows = slice(k * SUB, (k + 1) * SUB)
        for half, lanes in enumerate(halves):
            output[rows, lanes] = (inputs[rows, lanes].astype(F32) + row_total(0, k, half)).astype(BF16)

    def finish_in(k, copies):
        arrive(copies)
        rows = slice(k * SUB, (k + 1) * SUB)
        for half, lanes in enumerate(halves):
            d_norm[rows, lanes] = row_total(1, k, half)

    def weight_grad(left_of, right, wide_mask, target, stage, sems, first, last, reuse):
        def body(m, carry):
            at = pl.multiple_of(m * TILE, TILE)
            use = lax.rem(m, 2)

            def store():
                return pltpu.make_async_copy(stage.at[use], target.at[pl.ds(at, TILE), :], sems.at[use])

            if reuse:
                store().wait()
            else:
                @pl.when(m >= 2)
                def _():
                    store().wait()

            stage[use] = masked(tn_dot(left_of(at), right()), wide_mask[pl.ds(m * 4, 4)])
            store().start()
            return carry

        lax.fori_loop(first, last, body, 0)

    tokens = CHUNKS * 256

    def grad_down(first, last, reuse):
        weight_grad(
            lambda at: act[:, :, pl.ds(at, TILE)].reshape(tokens, TILE),
            lambda: cot[...].reshape(tokens, FEATS),
            ed, grad_w_down, stage_d, store_sem.at[0], first, last, reuse,
        )

    def grad_gate(first, last, reuse):
        weight_grad(
            lambda at: hid[:, :, :, :, pl.ds(at, TILE)].reshape(tokens, TILE),
            lambda: act[:, :, UNITS : 2 * UNITS].reshape(tokens, UNITS),
            eg, grad_w_gate, stage_u, store_sem.at[1], first, last, reuse,
        )

    all_job, out_job, in_job = (0, 3 * UNITS), (0, UNITS), (UNITS, 2 * UNITS)
    pd0 = mm_down_back(0)
    arrive(cot1[1])
    cot2.append(gather2(cot, 1))
    sd0 = scatter1(0, down_job, pd0)
    pg0 = mm_gate(0)
    pu0 = mm_up(0)
    arrive(hid1[1])
    hid2.append(gather2(hid, 1))
    sg0 = scatter1(0, gate_job, pg0)
    td0 = scatter2(0, down_job, sd0)
    su0 = scatter1(0, up_job, pu0)
    arrive(cot1[2])
    cot2.append(gather2(cot, 2))
    arrive(hid1[2])
    hid2.append(gather2(hid, 2))
    pd1 = mm_down_back(1)
    tg0 = scatter2(0, gate_job, sg0)
    pg1 = mm_gate(1) + mm_up(1)
    tu0 = scatter2(0, up_job, su0)
    sd1 = scatter1(1, down_job, pd1)
    sg1 = scatter1(1, gate_up_job, pg1)
    pd2 = mm_down_back(2)
    pg2 = mm_gate(2) + mm_up(2)
    for k in range(CHUNKS):
        keep(hid.at[k], hid_all.at[k])
    td1 = scatter2(1, down_job, sd1)
    activate(0, td0 + tg0 + tu0)
    a0 = spread1(0, all_job)
    sd2 = scatter1(2, down_job, pd2)
    tg1 = scatter2(1, gate_up_job, sg1)
    sg2 = scatter1(2, gate_up_job, pg2)
    h0, q0 = spread2(0, all_job, a0)
    activate(1, td1 + tg1)
    a1 = spread1(1, all_job)
    td2 = scatter2(2, down_job, sd2)
    r0 = spread3(0, all_job, h0, q0)
    tg2 = scatter2(2, gate_up_job, sg2)
    h1, q1 = spread2(1, all_job, a1)
    n0 = mm_in_back(0, r0)
    o0 = mm_out(0, ())
    activate(2, td2 + tg2)
    a2 = spread1(2, in_job)
    b2 = spread1(2, out_job)
    r1 = spread3(1, all_job, h1, q1)
    n0 = row_scatters2(1, 0, n0)
    o0 = row_scatters2(0, 0, o0)
    h2, q2 = spread2(2, in_job, a2)
    u2, v2 = spread2(2, out_job, b2)
    n1 = mm_in_back(1, r1)
    o1 = mm_out(1, ())
    finish_out(0, o0)
    finish_in(0, n0)
    r2 = spread3(2, in_job, h2, q2)
    n1 = row_scatters2(1, 1, n1)
    o1 = row_scatters2(0, 1, o1)
    n2 = mm_in_back(2, r2)
    w2 = spread3(2, out_job, u2, v2)
    finish_out(1, o1)
    finish_in(1, n1)
    grad_gate(0, 1, False)
    o2 = mm_out(2, w2)
    n2 = row_scatters2(1, 2, n2)
    grad_gate(1, 2, False)
    o2 = row_scatters2(0, 2, o2)
    finish_in(2, n2)

    moved = d_norm[...] * normed[...]
    in_own[...] = lane_fold(moved * gain[...])
    inner = all_col(in_own, in_in)
    gn_own[...] = jnp.sum(moved, axis=0, keepdims=True)
    gains = [send(gn_own, gn_in.at[index], device) for index, device in enumerate(row_peers)]
    grad_gate(2, 4, True)
    finish_out(2, o2)
    grad_down(0, 1, False)
    arrive(inner)
    inner_all = in_own[...]
    for index in range(7):
        inner_all = inner_all + in_in[index]
    row_inner = jnp.sum(inner_all, axis=1, keepdims=True) / D
    grad_inputs[...] = (
        grad_out[...].astype(F32)
        + inv_rms[:, 0:1] * (d_norm[...] * gain[...] - normed[...] * row_inner)
    ).astype(BF16)
    arrive(gains)
    gain_total = gn_own[...]
    for index in range(15):
        gain_total = gain_total + gn_in[index]
    grad_gain[...] = gain_total
    grad_down(1, 7, False)
    for use in range(2):
        pltpu.make_async_copy(stage_d.at[use], grad_w_down.at[pl.ds(0, TILE), :], store_sem.at[0, use]).wait()
        pltpu.make_async_copy(stage_u.at[use], grad_w_gate.at[pl.ds(0, TILE), :], store_sem.at[1, use]).wait()
    for copy in kept:
        copy.wait()
    for copy in started:
        copy.wait_send()


def last_grad(
    output_in, grad_inputs_in, grad_gain_in, grad_w_gate_in, grad_w_down_in, d_up_all, hid_all, mask_up,
    output, grad_inputs, grad_gain, grad_w_gate, grad_w_up, grad_w_down,
    d_up, hid, eu, small_a, small_b, small_c, big_a, big_b, stage, need_sem, in_sem, out_sem,
):
    needs = [
        pltpu.make_async_copy(d_up_all, d_up, need_sem.at[0]),
        pltpu.make_async_copy(hid_all, hid, need_sem.at[1]),
    ]
    for need in needs:
        need.start()
    moves = [
        (output_in, small_a, output, slice(0, LOCAL)),
        (grad_inputs_in, small_b, grad_inputs, slice(0, LOCAL)),
        (grad_gain_in, small_c, grad_gain, slice(0, 1)),
    ]
    for source, held, target in ((grad_w_gate_in, big_a, grad_w_gate), (grad_w_down_in, big_b, grad_w_down)):
        rows = source.shape[0] // 4
        moves += [(source, held, target, slice(n * rows, (n + 1) * rows)) for n in range(4)]
    loads, saves = [], []
    for index, (source, held, target, rows) in enumerate(moves):
        loads.append(pltpu.make_async_copy(source.at[rows, :], held.at[rows, :], in_sem.at[index]))
        loads[-1].start()

    def move(count):
        for _ in range(count):
            index = len(saves)
            source, held, target, rows = moves[index]
            loads[index].wait()
            saves.append(pltpu.make_async_copy(held.at[rows, :], target.at[rows, :], out_sem.at[index]))
            saves[-1].start()

    widen(mask_up[...], eu)
    for need in needs:
        need.wait()
    grads = []
    tokens = CHUNKS * 256
    for m in range(FEATS // TILE):
        rows = slice(m * TILE, (m + 1) * TILE)
        product = tn_dot(
            hid[:, :, :, :, rows].reshape(tokens, TILE), d_up[...].reshape(tokens, UNITS)
        )
        stage[m] = masked(product, eu[m * 4 : (m + 1) * 4])
        grads.append(pltpu.make_async_copy(stage.at[m], grad_w_up.at[rows, :], need_sem.at[m + 2]))
        grads[-1].start()
        move((2, 3, 3, 3)[m])
    for copy in saves + grads:
        copy.wait()


def shards(inputs, norm_gain, w_gate, w_up, w_down, mask_gate, mask_up, mask_down, grad_out):
    vmem = pl.BlockSpec(memory_space=pltpu.VMEM)
    anywhere = pl.BlockSpec(memory_space=pl.ANY)
    wide = 3 * UNITS
    shape = jax.ShapeDtypeStruct
    results = pl.pallas_call(
        layer,
        out_shape=(
            shape((LOCAL, FEATS), BF16),
            shape((LOCAL, FEATS), BF16),
            shape((1, FEATS), F32),
            shape((FEATS, UNITS), BF16),
            shape((UNITS, FEATS), BF16),
            shape((CHUNKS, 256, UNITS), BF16),
            shape((CHUNKS, 4, 4, SUB, FEATS), BF16),
        ),
        in_specs=[vmem, vmem, anywhere, anywhere, anywhere, vmem, vmem, vmem, vmem],
        out_specs=(vmem, vmem, vmem, anywhere, anywhere, anywhere, anywhere),
        scratch_shapes=[
            pltpu.VMEM((FEATS, UNITS), BF16),
            pltpu.VMEM((FEATS, UNITS), BF16),
            pltpu.VMEM((UNITS, FEATS), BF16),
            pltpu.VMEM((FEATS // BLOCK, SUB, UNITS), BF16),
            pltpu.VMEM((FEATS // BLOCK, SUB, UNITS), BF16),
            pltpu.VMEM((UNITS // BLOCK, SUB, FEATS), BF16),
            pltpu.VMEM((CHUNKS, 4, 4, SUB, FEATS), BF16),
            pltpu.VMEM((CHUNKS, 4, 4, SUB, FEATS), BF16),
            pltpu.VMEM((CHUNKS, 256, wide), BF16),
            pltpu.VMEM((CHUNKS, 128, wide), BF16),
            pltpu.VMEM((CHUNKS, SUB, wide), BF16),
            pltpu.VMEM((CHUNKS, SUB, wide), BF16),
            pltpu.VMEM((CHUNKS, 32, wide), BF16),
            pltpu.VMEM((CHUNKS, 32, wide), BF16),
            pltpu.VMEM((CHUNKS, 256, wide), BF16),
            pltpu.VMEM((2, CHUNKS, 4, 4, SUB, FEATS), BF16),
            pltpu.VMEM((2, CHUNKS, 3, 4, SUB, FEATS), BF16),
            pltpu.VMEM((2, CHUNKS, 4, SUB, FEATS), BF16),
            pltpu.VMEM((2, CHUNKS, 3, SUB, FEATS), BF16),
            pltpu.VMEM((LOCAL, FEATS), F32),
            pltpu.VMEM((LOCAL, 128), F32),
            pltpu.VMEM((LOCAL, FEATS), F32),
            pltpu.VMEM((LOCAL, 128), F32),
            pltpu.VMEM((7, LOCAL, 128), F32),
            pltpu.VMEM((LOCAL, 128), F32),
            pltpu.VMEM((7, LOCAL, 128), F32),
            pltpu.VMEM((1, FEATS), F32),
            pltpu.VMEM((15, 1, FEATS), F32),
            pltpu.VMEM((2, TILE, FEATS), BF16),
            pltpu.VMEM((2, TILE, UNITS), BF16),
            pltpu.SemaphoreType.DMA((COPIES,)),
            pltpu.SemaphoreType.DMA((COPIES,)),
            pltpu.SemaphoreType.DMA((3,)),
            pltpu.SemaphoreType.DMA((2, 2)),
            pltpu.SemaphoreType.DMA((2 * CHUNKS,)),
        ],
        compiler_params=pltpu.CompilerParams(
            collective_id=0, has_side_effects=True, vmem_limit_bytes=60 << 20
        ),
        name="layer",
    )(
        inputs, norm_gain.reshape(1, FEATS), w_gate, w_up, w_down,
        mask_gate, mask_up, mask_down.T, grad_out,
    )
    output, grad_inputs, grad_gain, grad_w_gate, grad_w_up, grad_w_down = pl.pallas_call(
        last_grad,
        out_shape=(
            shape((LOCAL, FEATS), BF16),
            shape((LOCAL, FEATS), BF16),
            shape((1, FEATS), F32),
            shape((FEATS, UNITS), BF16),
            shape((FEATS, UNITS), BF16),
            shape((UNITS, FEATS), BF16),
        ),
        in_specs=[anywhere] * 7 + [vmem],
        out_specs=(anywhere,) * 6,
        scratch_shapes=[
            pltpu.VMEM((CHUNKS, 256, UNITS), BF16),
            pltpu.VMEM((CHUNKS, 4, 4, SUB, FEATS), BF16),
            pltpu.VMEM((FEATS // BLOCK, SUB, UNITS), BF16),
            pltpu.VMEM((LOCAL, FEATS), BF16),
            pltpu.VMEM((LOCAL, FEATS), BF16),
            pltpu.VMEM((1, FEATS), F32),
            pltpu.VMEM((FEATS, UNITS), BF16),
            pltpu.VMEM((UNITS, FEATS), BF16),
            pltpu.VMEM((4, TILE, UNITS), BF16),
            pltpu.SemaphoreType.DMA((6,)),
            pltpu.SemaphoreType.DMA((11,)),
            pltpu.SemaphoreType.DMA((11,)),
        ],
        compiler_params=pltpu.CompilerParams(vmem_limit_bytes=60 << 20),
        name="last_grad",
    )(*results, mask_up)
    return output, grad_inputs, grad_gain.reshape(FEATS), grad_w_gate, grad_w_up, grad_w_down


def solution(mesh):
    in_specs = (
        P("row", "col"),
        P("col"),
        P("col", "row"),
        P("col", "row"),
        P("row", "col"),
        P("col", "row"),
        P("col", "row"),
        P("row", "col"),
        P("row", "col"),
    )
    out_specs = (
        P("row", "col"),
        P("row", "col"),
        P("col"),
        P("col", "row"),
        P("col", "row"),
        P("row", "col"),
    )
    return jax.shard_map(shards, mesh=mesh, in_specs=in_specs, out_specs=out_specs, check_vma=False)
```

```python
import functools

import jax
import jax.numpy as jnp
from jax import lax
from jax.experimental import pallas as pl
from jax.experimental.pallas import tpu as pltpu
from jax.sharding import PartitionSpec as P

D = 8192
BLOCK = 64
EPSILON = 1e-05
MESH = pl.DeviceIdType.MESH
F32 = jnp.float32
BF16 = jnp.bfloat16

LOCAL = 48
CHUNKS = 3
SUB = 16
FEATS = 1024
UNITS = 1792
HALF = FEATS // 2
TILE = 256
COPIES = 320


def nt_dot(left, right):
    return lax.dot_general(left, right, (((1,), (1,)), ((), ())), preferred_element_type=F32)


def nn_dot(left, right):
    return lax.dot_general(left, right, (((1,), (0,)), ((), ())), preferred_element_type=F32)


def tn_dot(left, right):
    return lax.dot_general(left, right, (((0,), (0,)), ((), ())), preferred_element_type=F32)


def masked(product, wide_mask):
    rows, width = product.shape
    blocks = product.astype(BF16).reshape(rows // BLOCK, BLOCK // SUB, SUB, width)
    return (blocks * wide_mask.reshape(rows // BLOCK, 1, SUB, width)).reshape(rows, width)


def lane_fold(value):
    total = value[:, 0:128]
    for start in range(128, value.shape[1], 128):
        total = total + value[:, start : start + 128]
    return total


def widen(mask, into):
    rows, blocks = mask.shape
    width = blocks * BLOCK
    unit = lax.broadcasted_iota(jnp.int32, (blocks, width), 1)
    first = lax.broadcasted_iota(jnp.int32, (blocks, width), 0) * BLOCK
    spread = jnp.where((unit >= first) & (unit < first + BLOCK), 1.0, 0.0).astype(BF16)
    wide_mask = nn_dot(mask.astype(F32).astype(BF16), spread)
    for r in range(rows):
        into[r] = jnp.broadcast_to(wide_mask[r : r + 1, :], (SUB, width)).astype(BF16)


def layer(
    inputs, gain, w_gate, w_up, w_down, mask_gate, mask_up, mask_down, grad_out,
    output, grad_inputs, grad_gain, grad_w_gate, grad_w_down, d_up_all, hid_all,
    gate_early, down_early, wg, wu, wd, eg, eu, ed, hid, cot, part, pair, fwd_a, fwd_b, from_l, from_r, act,
    row_part, row_in1, row_sum, row_in2, normed, inv_rms, d_norm,
    sq_own, sq_in, in_own, in_in, gn_own, gn_in, stage_d, stage_u,
    send_sem, recv_sem, load_sem, store_sem, keep_sem,
):
    row = lax.axis_index("row")
    col = lax.axis_index("col")
    y, z = row // 4, lax.rem(row, 4)
    x, core = col // 2, lax.rem(col, 2)

    def up(value, steps):
        return lax.rem(value + steps, 4)

    def at_x(steps, other=0):
        return (row, up(x, steps) * 2 + (1 - core if other else core))

    def at_y(steps):
        return (up(y, steps) * 4 + z, col)

    def at_z(steps):
        return (y * 4 + up(z, steps), col)

    partner = at_x(0, 1)
    started = []

    def send(src, dst, device):
        index = len(started)
        copy = pltpu.make_async_remote_copy(
            src_ref=src, dst_ref=dst, send_sem=send_sem.at[index], recv_sem=recv_sem.at[index],
            device_id=device, device_id_type=MESH,
        )
        copy.start()
        started.append(copy)
        return copy

    kept = []

    def keep(source, target):
        copy = pltpu.make_async_copy(source, target, keep_sem.at[len(kept)])
        copy.start()
        kept.append(copy)

    def arrive(copies):
        for copy in copies:
            copy.wait_recv()

    loads = [
        pltpu.make_async_copy(source, target, load_sem.at[index])
        for index, (source, target) in enumerate(((w_down, wd), (w_gate, wg), (w_up, wu)))
    ]
    for load in loads:
        load.start()

    barrier = pltpu.get_barrier_semaphore()
    row_peers = [
        (up(y, steps // 4) * 4 + up(z, steps % 4), col) for steps in range(1, 16)
    ]
    neighbours = [partner] + row_peers
    for steps in (1, 2, 3):
        neighbours += [at_x(steps), at_x(steps, 1)]
    for device in neighbours:
        pl.semaphore_signal(barrier, inc=1, device_id=device, device_id_type=MESH)

    for k in range(CHUNKS):
        cot[k, y, z] = grad_out[k * SUB : (k + 1) * SUB, :]
    wide = inputs[...].astype(F32)
    sq_own[...] = lane_fold(wide * wide)

    pl.semaphore_wait(barrier, len(neighbours))

    def all_col(own, into):
        copies = [send(own, into.at[0], partner)]
        for steps in (1, 2, 3):
            copies.append(send(own, into.at[2 * steps - 1], at_x(steps)))
            copies.append(send(own, into.at[2 * steps], at_x(steps, 1)))
        return copies

    def gather1(ref, k):
        copies = []
        for steps in (1, 2, 3):
            part_a = ref.at[k, y, z, :, pl.ds(0, HALF)]
            part_b = ref.at[k, y, z, :, pl.ds(HALF, HALF)]
            copies.append(send(part_a, part_a, at_z(steps)))
            copies.append(send(part_b, part_b, at_y(steps)))
        return copies

    def gather2(ref, k):
        copies = []
        for steps in (1, 2, 3):
            part_a = ref.at[k, y, :, :, pl.ds(0, HALF)]
            part_b = ref.at[k, :, z, :, pl.ds(HALF, HALF)]
            copies.append(send(part_a, part_a, at_y(steps)))
            copies.append(send(part_b, part_b, at_z(steps)))
        return copies

    cot1 = [gather1(cot, 0)]
    squares = all_col(sq_own, sq_in)

    def mask_weights(ref, wide_mask, load):
        load.wait()

        def body(r, carry):
            kept = wide_mask[r]
            for piece in range(BLOCK // SUB):
                rows = pl.ds(pl.multiple_of(r * BLOCK + piece * SUB, SUB), SUB)
                ref[rows, :] = ref[rows, :] * kept
            return carry

        lax.fori_loop(0, wide_mask.shape[0], body, 0)

    widen(mask_down[...].astype(F32).T, ed)
    arrive(cot1[0])
    cot2 = [gather2(cot, 0)]

    arrive(squares)
    squares_all = sq_own[...]
    for index in range(7):
        squares_all = squares_all + sq_in[index]
    inv_rms[...] = jnp.broadcast_to(
        lax.rsqrt(jnp.sum(squares_all, axis=1, keepdims=True) / D + EPSILON), (LOCAL, 128)
    )
    hid1 = []
    for k in range(CHUNKS):
        rows = slice(k * SUB, (k + 1) * SUB)
        normed[rows, :] = inputs[rows, :].astype(F32) * inv_rms[rows, 0:1]
        hid[k, y, z] = (normed[rows, :] * gain[...]).astype(BF16)
        if k == 0:
            hid1.append(gather1(hid, 0))
    mask_weights(wd, ed, loads[0])
    arrive(hid1[0])
    hid2 = [gather2(hid, 0)]
    for k in (1, 2):
        cot1.append(gather1(cot, k))
        hid1.append(gather1(hid, k))
    widen(mask_gate[...], eg)
    widen(mask_up[...], eu)
    mask_weights(wg, eg, loads[1])

    def chunk_of(ref, k):
        return ref[k].reshape(4 * 4 * SUB, FEATS)

    def tiles(count, body):
        def step(n, carry):
            body(pl.multiple_of(n * TILE, TILE))
            return carry

        lax.fori_loop(0, count, step, 0)

    def pair_send(k, start, width):
        return [
            send(
                part.at[k, pl.ds(pl.multiple_of((1 - core) * 128, 128), 128), pl.ds(start, width)],
                pair.at[k, :, pl.ds(start, width)],
                partner,
            )
        ]

    def mm_down_back(k):
        arrive(cot2[k])
        copies = []
        for start in (0, UNITS // 2):
            rows = slice(start, start + UNITS // 2)
            part[k, :, rows] = nt_dot(chunk_of(cot, k), wd[rows, :]).astype(BF16)
            copies += pair_send(k, start, UNITS // 2)
        return copies

    def mm_gate(k):
        arrive(hid2[k])
        part[k, :, UNITS : 2 * UNITS] = nn_dot(chunk_of(hid, k), wg[...]).astype(BF16)
        return pair_send(k, UNITS, UNITS)

    def mm_up(k):
        part[k, :, 2 * UNITS : 3 * UNITS] = nn_dot(chunk_of(hid, k), wu[...]).astype(BF16)
        return pair_send(k, 2 * UNITS, UNITS)

    def block_rows(which, offset, count):
        return pl.ds(pl.multiple_of(which * 32 + offset, SUB), count)

    def scatter1(k, job, copies):
        start, width = job
        cols = pl.ds(start, width)
        arrive(copies)
        mine = pl.multiple_of(core * 128, 128)
        def body(r, carry):
            rows = pl.ds(pl.multiple_of(r * SUB, SUB), SUB)
            own = part[k, pl.ds(pl.multiple_of(mine + r * SUB, SUB), SUB), cols].astype(F32)
            pair[k, rows, cols] = (own + pair[k, rows, cols].astype(F32)).astype(BF16)
            return carry
        lax.fori_loop(0, 8, body, 0)
        right, left = at_x(1), at_x(3)
        two = up(x, 2)
        return (
            send(pair.at[k, block_rows(two, 0, SUB), cols], fwd_a.at[k, :, cols], right),
            send(pair.at[k, block_rows(two, SUB, SUB), cols], fwd_b.at[k, :, cols], left),
            send(pair.at[k, block_rows(up(x, 1), SUB, SUB), cols], from_l.at[k, pl.ds(SUB, SUB), cols], right),
            send(pair.at[k, block_rows(up(x, 3), 0, SUB), cols], from_r.at[k, pl.ds(0, SUB), cols], left),
        )

    def scatter2(k, job, copies):
        start, width = job
        cols = pl.ds(start, width)
        right, left = at_x(1), at_x(3)
        arrive(copies[0:1])
        own = pair[k, block_rows(up(x, 1), 0, SUB), cols].astype(F32)
        fwd_a[k, :, cols] = (own + fwd_a[k, :, cols].astype(F32)).astype(BF16)
        first = send(fwd_a.at[k, :, cols], from_l.at[k, pl.ds(0, SUB), cols], right)
        arrive(copies[1:2])
        own = pair[k, block_rows(up(x, 3), SUB, SUB), cols].astype(F32)
        fwd_b[k, :, cols] = (own + fwd_b[k, :, cols].astype(F32)).astype(BF16)
        second = send(fwd_b.at[k, :, cols], from_r.at[k, pl.ds(SUB, SUB), cols], left)
        return (copies[2], copies[3], first, second)

    down_job, gate_up_job = (0, UNITS), (UNITS, 2 * UNITS)
    gate_job, up_job = (UNITS, UNITS), (2 * UNITS, UNITS)
    owner = core * 4 + x

    def activate(k, copies):
        arrive(copies)
        def total(start):
            cols = pl.ds(start, 256)
            return (
                pair[k, block_rows(x, 0, 32), cols].astype(F32)
                + from_l[k, :, cols].astype(F32)
                + from_r[k, :, cols].astype(F32)
            )

        def body(at):
            d_hidden = total(at)
            gate_value = total(UNITS + at)
            up_value = total(2 * UNITS + at)
            sigma = jax.nn.sigmoid(gate_value)
            silu = gate_value * sigma
            rows = block_rows(owner, 0, 32)
            act[k, rows, pl.ds(at, 256)] = (silu * up_value).astype(BF16)
            act[k, rows, pl.ds(UNITS + at, 256)] = (
                d_hidden * up_value * sigma * (1.0 + gate_value * (1.0 - sigma))
            ).astype(BF16)
            act[k, rows, pl.ds(2 * UNITS + at, 256)] = (d_hidden * silu).astype(BF16)

        tiles(UNITS // 256, body)

    def spread1(k, job):
        block = act.at[k, block_rows(owner, 0, 32), pl.ds(*job)]
        return (
            send(block, block, at_x(1)),
            send(block, block, at_x(3)),
            send(block, block, partner),
        )

    def spread2(k, job, copies):
        cols = pl.ds(*job)
        from_left, from_right = core * 4 + up(x, 3), core * 4 + up(x, 1)
        arrive(copies[0:1])
        half = act.at[k, block_rows(from_left, 0, SUB), cols]
        block = act.at[k, block_rows(from_left, 0, 32), cols]
        first = send(half, half, at_x(1))
        first_pair = send(block, block, partner)
        arrive(copies[1:2])
        half = act.at[k, block_rows(from_right, SUB, SUB), cols]
        block = act.at[k, block_rows(from_right, 0, 32), cols]
        second = send(half, half, at_x(3))
        second_pair = send(block, block, partner)
        return (first, second), (copies[2], first_pair, second_pair)

    def spread3(k, job, halves, pairs):
        arrive(halves)
        block = act.at[k, block_rows(core * 4 + up(x, 2), 0, 32), pl.ds(*job)]
        return pairs + (send(block, block, partner),)

    halves = (slice(0, HALF), slice(HALF, FEATS))

    def row_scatter1(which, k, half):
        copies = []
        lanes = pl.ds(half * HALF, HALF)
        for steps in (1, 2, 3):
            into = row_in1.at[which, k, steps - 1, :, :, lanes]
            if half == 0:
                copies.append(send(row_part.at[which, k, up(y, steps), :, :, lanes], into, at_y(steps)))
            else:
                copies.append(send(row_part.at[which, k, :, up(z, steps), :, lanes], into, at_z(steps)))
        return copies

    def row_scatter2(which, k, half, copies):
        arrive(copies)
        lanes = halves[half]
        if half == 0:
            total = row_part[which, k, y, :, :, lanes].astype(F32)
        else:
            total = row_part[which, k, :, z, :, lanes].astype(F32)
        for index in range(3):
            total = total + row_in1[which, k, index, :, :, lanes].astype(F32)
        row_sum[which, k, :, :, lanes] = total.astype(BF16)
        after = []
        lanes = pl.ds(half * HALF, HALF)
        for steps in (1, 2, 3):
            into = row_in2.at[which, k, steps - 1, :, lanes]
            if half == 0:
                after.append(send(row_sum.at[which, k, up(z, steps), :, lanes], into, at_z(steps)))
            else:
                after.append(send(row_sum.at[which, k, up(y, steps), :, lanes], into, at_y(steps)))
        return after

    def row_scatters2(which, k, copies):
        return row_scatter2(which, k, 0, copies[0:3]) + row_scatter2(which, k, 1, copies[3:6])

    def row_total(which, k, half):
        lanes = halves[half]
        total = row_sum[which, k, y if half else z, :, lanes].astype(F32)
        for index in range(3):
            total = total + row_in2[which, k, index, :, lanes].astype(F32)
        return total

    def mm_out(k, pairs):
        arrive(pairs)
        product = nn_dot(act[k, :, 0:UNITS], wd[...]).astype(BF16)
        row_part[0, k] = product.reshape(4, 4, SUB, FEATS)
        return row_scatter1(0, k, 0) + row_scatter1(0, k, 1)

    def mm_in_back(k, pairs):
        arrive(pairs)
        keep(act.at[k, :, pl.ds(2 * UNITS, UNITS)], d_up_all.at[k])
        copies = []
        for half, lanes in enumerate(halves):
            product = nt_dot(act[k, :, UNITS : 2 * UNITS], wg[lanes, :]) + nt_dot(
                act[k, :, 2 * UNITS : 3 * UNITS], wu[lanes, :]
            )
            row_part[1, k, :, :, :, lanes] = product.astype(BF16).reshape(4, 4, SUB, HALF)
            copies += row_scatter1(1, k, half)
        return copies

    def finish_out(k, copies):
        arrive(copies)
        rows = slice(k * SUB, (k + 1) * SUB)
        for half, lanes in enumerate(halves):
            output[rows, lanes] = (inputs[rows, lanes].astype(F32) + row_total(0, k, half)).astype(BF16)

    def finish_in(k, copies):
        arrive(copies)
        rows = slice(k * SUB, (k + 1) * SUB)
        for half, lanes in enumerate(halves):
            d_norm[rows, lanes] = row_total(1, k, half)

    def early_grad(left_of, right, early, first, last):
        def body(m, carry):
            at = pl.multiple_of(m * TILE, TILE)
            early[m] = tn_dot(left_of(0, 2, at), right(0, 2)).astype(BF16)
            return carry

        lax.fori_loop(first, last, body, 0)

    def weight_grad(left_of, right, early, wide_mask, target, stage, sems, first, last, reuse):
        def body(m, carry):
            at = pl.multiple_of(m * TILE, TILE)
            use = lax.rem(m, 2)

            def store():
                return pltpu.make_async_copy(stage.at[use], target.at[pl.ds(at, TILE), :], sems.at[use])

            if reuse:
                store().wait()
            else:
                @pl.when(m >= 2)
                def _():
                    store().wait()

            product = tn_dot(left_of(2, 3, at), right(2, 3)) + early[m].astype(F32)
            stage[use] = masked(product, wide_mask[pl.ds(m * 4, 4)])
            store().start()
            return carry

        lax.fori_loop(first, last, body, 0)

    def act_of(start, width):
        def get(k0, k1):
            return act[k0:k1, :, start : start + width].reshape((k1 - k0) * 256, width)

        return get

    def act_left(k0, k1, at):
        return act[k0:k1, :, pl.ds(at, TILE)].reshape((k1 - k0) * 256, TILE)

    def cot_right(k0, k1):
        return cot[k0:k1].reshape((k1 - k0) * 256, FEATS)

    def hid_left(k0, k1, at):
        return hid[k0:k1, :, :, :, pl.ds(at, TILE)].reshape((k1 - k0) * 256, TILE)

    d_gate_right = act_of(UNITS, UNITS)

    def early_down(first, last):
        early_grad(act_left, cot_right, down_early, first, last)

    def early_gate(first, last):
        early_grad(hid_left, d_gate_right, gate_early, first, last)

    def grad_down(first, last, reuse):
        weight_grad(
            act_left, cot_right, down_early, ed, grad_w_down, stage_d, store_sem.at[0], first, last, reuse
        )

    def grad_gate(first, last, reuse):
        weight_grad(
            hid_left, d_gate_right, gate_early, eg, grad_w_gate, stage_u, store_sem.at[1], first, last, reuse
        )

    all_job, out_job, in_job = (0, 3 * UNITS), (0, UNITS), (UNITS, 2 * UNITS)
    pd0 = mm_down_back(0)
    arrive(cot1[1])
    cot2.append(gather2(cot, 1))
    sd0 = scatter1(0, down_job, pd0)
    pg0 = mm_gate(0)
    mask_weights(wu, eu, loads[2])
    pu0 = mm_up(0)
    arrive(hid1[1])
    hid2.append(gather2(hid, 1))
    sg0 = scatter1(0, gate_job, pg0)
    td0 = scatter2(0, down_job, sd0)
    su0 = scatter1(0, up_job, pu0)
    arrive(cot1[2])
    cot2.append(gather2(cot, 2))
    arrive(hid1[2])
    hid2.append(gather2(hid, 2))
    pd1 = mm_down_back(1)
    tg0 = scatter2(0, gate_job, sg0)
    pg1 = mm_gate(1) + mm_up(1)
    tu0 = scatter2(0, up_job, su0)
    sd1 = scatter1(1, down_job, pd1)
    sg1 = scatter1(1, gate_up_job, pg1)
    pd2 = mm_down_back(2)
    pg2 = mm_gate(2) + mm_up(2)
    for k in range(CHUNKS):
        keep(hid.at[k], hid_all.at[k])
    td1 = scatter2(1, down_job, sd1)
    activate(0, td0 + tg0 + tu0)
    a0 = spread1(0, all_job)
    sd2 = scatter1(2, down_job, pd2)
    tg1 = scatter2(1, gate_up_job, sg1)
    sg2 = scatter1(2, gate_up_job, pg2)
    h0, q0 = spread2(0, all_job, a0)
    activate(1, td1 + tg1)
    a1 = spread1(1, all_job)
    td2 = scatter2(2, down_job, sd2)
    r0 = spread3(0, all_job, h0, q0)
    tg2 = scatter2(2, gate_up_job, sg2)
    h1, q1 = spread2(1, all_job, a1)
    n0 = mm_in_back(0, r0)
    o0 = mm_out(0, ())
    activate(2, td2 + tg2)
    a2 = spread1(2, in_job)
    b2 = spread1(2, out_job)
    r1 = spread3(1, all_job, h1, q1)
    n0 = row_scatters2(1, 0, n0)
    o0 = row_scatters2(0, 0, o0)
    n1 = mm_in_back(1, r1)
    h2, q2 = spread2(2, in_job, a2)
    o1 = mm_out(1, ())
    early_gate(0, 2)
    u2, v2 = spread2(2, out_job, b2)
    early_gate(2, 4)
    r2 = spread3(2, in_job, h2, q2)
    n1 = row_scatters2(1, 1, n1)
    w2 = spread3(2, out_job, u2, v2)
    early_down(0, 3)
    n2 = mm_in_back(2, r2)
    o2 = mm_out(2, w2)
    o1 = row_scatters2(0, 1, o1)
    finish_out(0, o0)
    finish_in(0, n0)
    finish_in(1, n1)
    early_down(3, 7)
    n2 = row_scatters2(1, 2, n2)
    grad_gate(0, 2, False)
    o2 = row_scatters2(0, 2, o2)
    grad_gate(2, 4, True)
    finish_in(2, n2)

    moved = d_norm[...] * normed[...]
    in_own[...] = lane_fold(moved * gain[...])
    inner = all_col(in_own, in_in)
    gn_own[...] = jnp.sum(moved, axis=0, keepdims=True)
    gains = [send(gn_own, gn_in.at[index], device) for index, device in enumerate(row_peers)]
    finish_out(1, o1)
    grad_down(0, 4, False)
    finish_out(2, o2)
    arrive(inner)
    inner_all = in_own[...]
    for index in range(7):
        inner_all = inner_all + in_in[index]
    row_inner = jnp.sum(inner_all, axis=1, keepdims=True) / D
    grad_inputs[...] = (
        grad_out[...].astype(F32)
        + inv_rms[:, 0:1] * (d_norm[...] * gain[...] - normed[...] * row_inner)
    ).astype(BF16)
    arrive(gains)
    gain_total = gn_own[...]
    for index in range(15):
        gain_total = gain_total + gn_in[index]
    grad_gain[...] = gain_total
    grad_down(4, 7, True)
    for use in range(2):
        pltpu.make_async_copy(stage_d.at[use], grad_w_down.at[pl.ds(0, TILE), :], store_sem.at[0, use]).wait()
        pltpu.make_async_copy(stage_u.at[use], grad_w_gate.at[pl.ds(0, TILE), :], store_sem.at[1, use]).wait()
    for copy in kept:
        copy.wait()
    for copy in started:
        copy.wait_send()


def last_grad(
    output_in, grad_inputs_in, grad_gain_in, grad_w_gate_in, grad_w_down_in, d_up_all, hid_all, mask_up,
    output, grad_inputs, grad_gain, grad_w_gate, grad_w_up, grad_w_down,
    d_up, hid, eu, small_a, small_b, small_c, big_a, big_b, stage, need_sem, in_sem, out_sem,
):
    needs = [
        pltpu.make_async_copy(d_up_all, d_up, need_sem.at[0]),
        pltpu.make_async_copy(hid_all, hid, need_sem.at[1]),
    ]
    for need in needs:
        need.start()
    moves = [
        (output_in, small_a, output, slice(0, LOCAL)),
        (grad_inputs_in, small_b, grad_inputs, slice(0, LOCAL)),
        (grad_gain_in, small_c, grad_gain, slice(0, 1)),
    ]
    for source, held, target in ((grad_w_gate_in, big_a, grad_w_gate), (grad_w_down_in, big_b, grad_w_down)):
        rows = source.shape[0] // 4
        moves += [(source, held, target, slice(n * rows, (n + 1) * rows)) for n in range(4)]
    loads = [
        pltpu.make_async_copy(source.at[rows, :], held.at[rows, :], in_sem.at[index])
        for index, (source, held, target, rows) in enumerate(moves)
    ]
    saves = []

    def move(count):
        for _ in range(count):
            index = len(saves)
            source, held, target, rows = moves[index]
            loads[index].wait()
            saves.append(pltpu.make_async_copy(held.at[rows, :], target.at[rows, :], out_sem.at[index]))
            saves[-1].start()

    widen(mask_up[...], eu)
    for need in needs:
        need.wait()
    for load in loads:
        load.start()
    grads = []
    tokens = CHUNKS * 256
    for m in range(FEATS // TILE):
        rows = slice(m * TILE, (m + 1) * TILE)
        product = tn_dot(
            hid[:, :, :, :, rows].reshape(tokens, TILE), d_up[...].reshape(tokens, UNITS)
        )
        stage[m] = masked(product, eu[m * 4 : (m + 1) * 4])
        grads.append(pltpu.make_async_copy(stage.at[m], grad_w_up.at[rows, :], need_sem.at[m + 2]))
        grads[-1].start()
        move((2, 3, 3, 3)[m])
    for copy in saves + grads:
        copy.wait()


def shards(inputs, norm_gain, w_gate, w_up, w_down, mask_gate, mask_up, mask_down, grad_out):
    vmem = pl.BlockSpec(memory_space=pltpu.VMEM)
    anywhere = pl.BlockSpec(memory_space=pl.ANY)
    wide = 3 * UNITS
    shape = jax.ShapeDtypeStruct
    results = pl.pallas_call(
        layer,
        out_shape=(
            shape((LOCAL, FEATS), BF16),
            shape((LOCAL, FEATS), BF16),
            shape((1, FEATS), F32),
            shape((FEATS, UNITS), BF16),
            shape((UNITS, FEATS), BF16),
            shape((CHUNKS, 256, UNITS), BF16),
            shape((CHUNKS, 4, 4, SUB, FEATS), BF16),
        ),
        in_specs=[vmem, vmem, anywhere, anywhere, anywhere, vmem, vmem, vmem, vmem],
        out_specs=(vmem, vmem, vmem, anywhere, anywhere, anywhere, anywhere),
        scratch_shapes=[
            pltpu.VMEM((FEATS // TILE, TILE, UNITS), BF16),
            pltpu.VMEM((UNITS // TILE, TILE, FEATS), BF16),
            pltpu.VMEM((FEATS, UNITS), BF16),
            pltpu.VMEM((FEATS, UNITS), BF16),
            pltpu.VMEM((UNITS, FEATS), BF16),
            pltpu.VMEM((FEATS // BLOCK, SUB, UNITS), BF16),
            pltpu.VMEM((FEATS // BLOCK, SUB, UNITS), BF16),
            pltpu.VMEM((UNITS // BLOCK, SUB, FEATS), BF16),
            pltpu.VMEM((CHUNKS, 4, 4, SUB, FEATS), BF16),
            pltpu.VMEM((CHUNKS, 4, 4, SUB, FEATS), BF16),
            pltpu.VMEM((CHUNKS, 256, wide), BF16),
            pltpu.VMEM((CHUNKS, 128, wide), BF16),
            pltpu.VMEM((CHUNKS, SUB, wide), BF16),
            pltpu.VMEM((CHUNKS, SUB, wide), BF16),
            pltpu.VMEM((CHUNKS, 32, wide), BF16),
            pltpu.VMEM((CHUNKS, 32, wide), BF16),
            pltpu.VMEM((CHUNKS, 256, wide), BF16),
            pltpu.VMEM((2, CHUNKS, 4, 4, SUB, FEATS), BF16),
            pltpu.VMEM((2, CHUNKS, 3, 4, SUB, FEATS), BF16),
            pltpu.VMEM((2, CHUNKS, 4, SUB, FEATS), BF16),
            pltpu.VMEM((2, CHUNKS, 3, SUB, FEATS), BF16),
            pltpu.VMEM((LOCAL, FEATS), F32),
            pltpu.VMEM((LOCAL, 128), F32),
            pltpu.VMEM((LOCAL, FEATS), F32),
            pltpu.VMEM((LOCAL, 128), F32),
            pltpu.VMEM((7, LOCAL, 128), F32),
            pltpu.VMEM((LOCAL, 128), F32),
            pltpu.VMEM((7, LOCAL, 128), F32),
            pltpu.VMEM((1, FEATS), F32),
            pltpu.VMEM((15, 1, FEATS), F32),
            pltpu.VMEM((2, TILE, FEATS), BF16),
            pltpu.VMEM((2, TILE, UNITS), BF16),
            pltpu.SemaphoreType.DMA((COPIES,)),
            pltpu.SemaphoreType.DMA((COPIES,)),
            pltpu.SemaphoreType.DMA((3,)),
            pltpu.SemaphoreType.DMA((2, 2)),
            pltpu.SemaphoreType.DMA((2 * CHUNKS,)),
        ],
        compiler_params=pltpu.CompilerParams(
            collective_id=0, has_side_effects=True, vmem_limit_bytes=60 << 20
        ),
        name="layer",
    )(
        inputs, norm_gain.reshape(1, FEATS), w_gate, w_up, w_down,
        mask_gate, mask_up, mask_down.T, grad_out,
    )
    output, grad_inputs, grad_gain, grad_w_gate, grad_w_up, grad_w_down = pl.pallas_call(
        last_grad,
        out_shape=(
            shape((LOCAL, FEATS), BF16),
            shape((LOCAL, FEATS), BF16),
            shape((1, FEATS), F32),
            shape((FEATS, UNITS), BF16),
            shape((FEATS, UNITS), BF16),
            shape((UNITS, FEATS), BF16),
        ),
        in_specs=[anywhere] * 7 + [vmem],
        out_specs=(anywhere,) * 6,
        scratch_shapes=[
            pltpu.VMEM((CHUNKS, 256, UNITS), BF16),
            pltpu.VMEM((CHUNKS, 4, 4, SUB, FEATS), BF16),
            pltpu.VMEM((FEATS // BLOCK, SUB, UNITS), BF16),
            pltpu.VMEM((LOCAL, FEATS), BF16),
            pltpu.VMEM((LOCAL, FEATS), BF16),
            pltpu.VMEM((1, FEATS), F32),
            pltpu.VMEM((FEATS, UNITS), BF16),
            pltpu.VMEM((UNITS, FEATS), BF16),
            pltpu.VMEM((4, TILE, UNITS), BF16),
            pltpu.SemaphoreType.DMA((6,)),
            pltpu.SemaphoreType.DMA((11,)),
            pltpu.SemaphoreType.DMA((11,)),
        ],
        compiler_params=pltpu.CompilerParams(vmem_limit_bytes=60 << 20),
        name="last_grad",
    )(*results, mask_up)
    return output, grad_inputs, grad_gain.reshape(FEATS), grad_w_gate, grad_w_up, grad_w_down


def solution(mesh):
    in_specs = (
        P("row", "col"),
        P("col"),
        P("col", "row"),
        P("col", "row"),
        P("row", "col"),
        P("col", "row"),
        P("col", "row"),
        P("row", "col"),
        P("row", "col"),
    )
    out_specs = (
        P("row", "col"),
        P("row", "col"),
        P("col"),
        P("col", "row"),
        P("col", "row"),
        P("row", "col"),
    )
    return jax.shard_map(shards, mesh=mesh, in_specs=in_specs, out_specs=out_specs, check_vma=False)
```

```python
import functools

import jax
import jax.numpy as jnp
from jax import lax
from jax.experimental import pallas as pl
from jax.experimental.pallas import tpu as pltpu
from jax.sharding import PartitionSpec as P

D = 8192
BLOCK = 64
EPSILON = 1e-05
MESH = pl.DeviceIdType.MESH
F32 = jnp.float32
BF16 = jnp.bfloat16

LOCAL = 48
CHUNKS = 3
SUB = 16
FEATS = 1024
UNITS = 1792
HALF = FEATS // 2
TILE = 256
COPIES = 320


def nt_dot(left, right):
    return lax.dot_general(left, right, (((1,), (1,)), ((), ())), preferred_element_type=F32)


def nn_dot(left, right):
    return lax.dot_general(left, right, (((1,), (0,)), ((), ())), preferred_element_type=F32)


def tn_dot(left, right):
    return lax.dot_general(left, right, (((0,), (0,)), ((), ())), preferred_element_type=F32)


def masked(product, wide_mask):
    rows, width = product.shape
    blocks = product.astype(BF16).reshape(rows // BLOCK, BLOCK // SUB, SUB, width)
    return (blocks * wide_mask.reshape(rows // BLOCK, 1, SUB, width)).reshape(rows, width)


def lane_fold(value):
    total = value[:, 0:128]
    for start in range(128, value.shape[1], 128):
        total = total + value[:, start : start + 128]
    return total


def widen(mask, into):
    rows, blocks = mask.shape
    width = blocks * BLOCK
    unit = lax.broadcasted_iota(jnp.int32, (blocks, width), 1)
    first = lax.broadcasted_iota(jnp.int32, (blocks, width), 0) * BLOCK
    spread = jnp.where((unit >= first) & (unit < first + BLOCK), 1.0, 0.0).astype(BF16)
    wide_mask = nn_dot(mask.astype(F32).astype(BF16), spread)
    for r in range(rows):
        into[r] = jnp.broadcast_to(wide_mask[r : r + 1, :], (SUB, width)).astype(BF16)


def layer(
    inputs_at, gain_at, w_gate, w_up, w_down, mask_gate_at, mask_up_at, mask_down_at, grad_out_at,
    output_at, grad_inputs_at, grad_gain_at, grad_w_gate, grad_w_down, d_up_all, hid_all,
    inputs, gain, mask_gate, mask_up, mask_down, grad_out, output, grad_inputs, grad_gain,
    gate_early, down_early, wg, wu, wd, eg, eu, ed, hid, cot, part, pair, fwd_a, fwd_b, from_l, from_r, act,
    row_part, row_in1, row_sum, row_in2, normed, inv_rms, d_norm,
    sq_own, sq_in, in_own, in_in, gn_own, gn_in, stage_d, stage_u,
    send_sem, recv_sem, load_sem, store_sem, keep_sem, small_sem,
):
    row = lax.axis_index("row")
    col = lax.axis_index("col")
    y, z = row // 4, lax.rem(row, 4)
    x, core = col // 2, lax.rem(col, 2)

    def up(value, steps):
        return lax.rem(value + steps, 4)

    def at_x(steps, other=0):
        return (row, up(x, steps) * 2 + (1 - core if other else core))

    def at_y(steps):
        return (up(y, steps) * 4 + z, col)

    def at_z(steps):
        return (y * 4 + up(z, steps), col)

    partner = at_x(0, 1)
    started = []

    def send(src, dst, device):
        index = len(started)
        copy = pltpu.make_async_remote_copy(
            src_ref=src, dst_ref=dst, send_sem=send_sem.at[index], recv_sem=recv_sem.at[index],
            device_id=device, device_id_type=MESH,
        )
        copy.start()
        started.append(copy)
        return copy

    kept = []

    def keep(source, target):
        copy = pltpu.make_async_copy(source, target, keep_sem.at[len(kept)])
        copy.start()
        kept.append(copy)

    def arrive(copies):
        for copy in copies:
            copy.wait_recv()

    smalls = [
        pltpu.make_async_copy(source, target, small_sem.at[index])
        for index, (source, target) in enumerate((
            (grad_out_at, grad_out), (inputs_at, inputs), (gain_at, gain),
            (mask_down_at, mask_down), (mask_gate_at, mask_gate), (mask_up_at, mask_up),
        ))
    ]
    for small in smalls:
        small.start()

    barrier = pltpu.get_barrier_semaphore()
    row_peers = [
        (up(y, steps // 4) * 4 + up(z, steps % 4), col) for steps in range(1, 16)
    ]
    neighbours = [partner] + row_peers
    for steps in (1, 2, 3):
        neighbours += [at_x(steps), at_x(steps, 1)]
    for device in neighbours:
        pl.semaphore_signal(barrier, inc=1, device_id=device, device_id_type=MESH)

    loads = [
        pltpu.make_async_copy(source, target, load_sem.at[index])
        for index, (source, target) in enumerate(((w_down, wd), (w_gate, wg), (w_up, wu)))
    ]
    loads[0].start()

    for small in smalls:
        small.wait()
    for k in range(CHUNKS):
        cot[k, y, z] = grad_out[k * SUB : (k + 1) * SUB, :]
    wide = inputs[...].astype(F32)
    sq_own[...] = lane_fold(wide * wide)

    pl.semaphore_wait(barrier, len(neighbours))

    def all_col(own, into):
        copies = [send(own, into.at[0], partner)]
        for steps in (1, 2, 3):
            copies.append(send(own, into.at[2 * steps - 1], at_x(steps)))
            copies.append(send(own, into.at[2 * steps], at_x(steps, 1)))
        return copies

    def gather1(ref, k):
        copies = []
        for steps in (1, 2, 3):
            part_a = ref.at[k, y, z, :, pl.ds(0, HALF)]
            part_b = ref.at[k, y, z, :, pl.ds(HALF, HALF)]
            copies.append(send(part_a, part_a, at_z(steps)))
            copies.append(send(part_b, part_b, at_y(steps)))
        return copies

    def gather2(ref, k):
        copies = []
        for steps in (1, 2, 3):
            part_a = ref.at[k, y, :, :, pl.ds(0, HALF)]
            part_b = ref.at[k, :, z, :, pl.ds(HALF, HALF)]
            copies.append(send(part_a, part_a, at_y(steps)))
            copies.append(send(part_b, part_b, at_z(steps)))
        return copies

    cot1 = [gather1(cot, 0)]
    squares = all_col(sq_own, sq_in)

    def mask_weights(ref, wide_mask, load):
        load.wait()

        def body(r, carry):
            kept = wide_mask[r]
            for piece in range(BLOCK // SUB):
                rows = pl.ds(pl.multiple_of(r * BLOCK + piece * SUB, SUB), SUB)
                ref[rows, :] = ref[rows, :] * kept
            return carry

        lax.fori_loop(0, wide_mask.shape[0], body, 0)

    widen(mask_down[...].astype(F32).T, ed)
    widen(mask_gate[...], eg)
    widen(mask_up[...], eu)
    arrive(cot1[0])
    cot2 = [gather2(cot, 0)]

    arrive(squares)
    squares_all = sq_own[...]
    for index in range(7):
        squares_all = squares_all + sq_in[index]
    inv_rms[...] = jnp.broadcast_to(
        lax.rsqrt(jnp.sum(squares_all, axis=1, keepdims=True) / D + EPSILON), (LOCAL, 128)
    )
    hid1 = []
    for k in range(CHUNKS):
        rows = slice(k * SUB, (k + 1) * SUB)
        normed[rows, :] = inputs[rows, :].astype(F32) * inv_rms[rows, 0:1]
        hid[k, y, z] = (normed[rows, :] * gain[...]).astype(BF16)
        if k == 0:
            hid1.append(gather1(hid, 0))
            loads[1].start()
            loads[2].start()
    mask_weights(wd, ed, loads[0])
    arrive(hid1[0])
    hid2 = [gather2(hid, 0)]
    cot1.append(gather1(cot, 1))

    def chunk_of(ref, k):
        return ref[k].reshape(4 * 4 * SUB, FEATS)

    def tiles(count, body):
        def step(n, carry):
            body(pl.multiple_of(n * TILE, TILE))
            return carry

        lax.fori_loop(0, count, step, 0)

    def pair_send(k, start, width):
        return [
            send(
                part.at[k, pl.ds(pl.multiple_of((1 - core) * 128, 128), 128), pl.ds(start, width)],
                pair.at[k, :, pl.ds(start, width)],
                partner,
            )
        ]

    def mm_down_back(k):
        arrive(cot2[k])
        copies = []
        for start in (0, UNITS // 2):
            rows = slice(start, start + UNITS // 2)
            part[k, :, rows] = nt_dot(chunk_of(cot, k), wd[rows, :]).astype(BF16)
            copies += pair_send(k, start, UNITS // 2)
        return copies

    def mm_gate(k):
        arrive(hid2[k])
        part[k, :, UNITS : 2 * UNITS] = nn_dot(chunk_of(hid, k), wg[...]).astype(BF16)
        return pair_send(k, UNITS, UNITS)

    def mm_up(k):
        part[k, :, 2 * UNITS : 3 * UNITS] = nn_dot(chunk_of(hid, k), wu[...]).astype(BF16)
        return pair_send(k, 2 * UNITS, UNITS)

    def block_rows(which, offset, count):
        return pl.ds(pl.multiple_of(which * 32 + offset, SUB), count)

    def scatter1(k, job, copies):
        start, width = job
        cols = pl.ds(start, width)
        arrive(copies)
        mine = pl.multiple_of(core * 128, 128)
        def body(r, carry):
            rows = pl.ds(pl.multiple_of(r * SUB, SUB), SUB)
            own = part[k, pl.ds(pl.multiple_of(mine + r * SUB, SUB), SUB), cols].astype(F32)
            pair[k, rows, cols] = (own + pair[k, rows, cols].astype(F32)).astype(BF16)
            return carry
        lax.fori_loop(0, 8, body, 0)
        right, left = at_x(1), at_x(3)
        two = up(x, 2)
        return (
            send(pair.at[k, block_rows(two, 0, SUB), cols], fwd_a.at[k, :, cols], right),
            send(pair.at[k, block_rows(two, SUB, SUB), cols], fwd_b.at[k, :, cols], left),
            send(pair.at[k, block_rows(up(x, 1), SUB, SUB), cols], from_l.at[k, pl.ds(SUB, SUB), cols], right),
            send(pair.at[k, block_rows(up(x, 3), 0, SUB), cols], from_r.at[k, pl.ds(0, SUB), cols], left),
        )

    def scatter2(k, job, copies):
        start, width = job
        cols = pl.ds(start, width)
        right, left = at_x(1), at_x(3)
        arrive(copies[0:1])
        own = pair[k, block_rows(up(x, 1), 0, SUB), cols].astype(F32)
        fwd_a[k, :, cols] = (own + fwd_a[k, :, cols].astype(F32)).astype(BF16)
        first = send(fwd_a.at[k, :, cols], from_l.at[k, pl.ds(0, SUB), cols], right)
        arrive(copies[1:2])
        own = pair[k, block_rows(up(x, 3), SUB, SUB), cols].astype(F32)
        fwd_b[k, :, cols] = (own + fwd_b[k, :, cols].astype(F32)).astype(BF16)
        second = send(fwd_b.at[k, :, cols], from_r.at[k, pl.ds(SUB, SUB), cols], left)
        return (copies[2], copies[3], first, second)

    down_job, gate_up_job = (0, UNITS), (UNITS, 2 * UNITS)
    gate_job, up_job = (UNITS, UNITS), (2 * UNITS, UNITS)
    owner = core * 4 + x

    def activate(k, copies):
        arrive(copies)
        def total(start):
            cols = pl.ds(start, 256)
            return (
                pair[k, block_rows(x, 0, 32), cols].astype(F32)
                + from_l[k, :, cols].astype(F32)
                + from_r[k, :, cols].astype(F32)
            )

        def body(at):
            d_hidden = total(at)
            gate_value = total(UNITS + at)
            up_value = total(2 * UNITS + at)
            sigma = jax.nn.sigmoid(gate_value)
            silu = gate_value * sigma
            rows = block_rows(owner, 0, 32)
            act[k, rows, pl.ds(at, 256)] = (silu * up_value).astype(BF16)
            act[k, rows, pl.ds(UNITS + at, 256)] = (
                d_hidden * up_value * sigma * (1.0 + gate_value * (1.0 - sigma))
            ).astype(BF16)
            act[k, rows, pl.ds(2 * UNITS + at, 256)] = (d_hidden * silu).astype(BF16)

        tiles(UNITS // 256, body)

    def spread1(k, job):
        block = act.at[k, block_rows(owner, 0, 32), pl.ds(*job)]
        return (
            send(block, block, at_x(1)),
            send(block, block, at_x(3)),
            send(block, block, partner),
        )

    def spread2(k, job, copies):
        cols = pl.ds(*job)
        from_left, from_right = core * 4 + up(x, 3), core * 4 + up(x, 1)
        arrive(copies[0:1])
        half = act.at[k, block_rows(from_left, 0, SUB), cols]
        block = act.at[k, block_rows(from_left, 0, 32), cols]
        first = send(half, half, at_x(1))
        first_pair = send(block, block, partner)
        arrive(copies[1:2])
        half = act.at[k, block_rows(from_right, SUB, SUB), cols]
        block = act.at[k, block_rows(from_right, 0, 32), cols]
        second = send(half, half, at_x(3))
        second_pair = send(block, block, partner)
        return (first, second), (copies[2], first_pair, second_pair)

    def spread3(k, job, halves, pairs):
        arrive(halves)
        block = act.at[k, block_rows(core * 4 + up(x, 2), 0, 32), pl.ds(*job)]
        return pairs + (send(block, block, partner),)

    halves = (slice(0, HALF), slice(HALF, FEATS))

    def row_scatter1(which, k, half, start=0, width=HALF):
        copies = []
        lanes = pl.ds(half * HALF + start, width)
        for steps in (1, 2, 3):
            into = row_in1.at[which, k, steps - 1, :, :, lanes]
            if half == 0:
                copies.append(send(row_part.at[which, k, up(y, steps), :, :, lanes], into, at_y(steps)))
            else:
                copies.append(send(row_part.at[which, k, :, up(z, steps), :, lanes], into, at_z(steps)))
        return copies

    def row_scatter2(which, k, half, copies):
        arrive(copies)
        lanes = halves[half]
        if half == 0:
            total = row_part[which, k, y, :, :, lanes].astype(F32)
        else:
            total = row_part[which, k, :, z, :, lanes].astype(F32)
        for index in range(3):
            total = total + row_in1[which, k, index, :, :, lanes].astype(F32)
        row_sum[which, k, :, :, lanes] = total.astype(BF16)
        after = []
        lanes = pl.ds(half * HALF, HALF)
        for steps in (1, 2, 3):
            into = row_in2.at[which, k, steps - 1, :, lanes]
            if half == 0:
                after.append(send(row_sum.at[which, k, up(z, steps), :, lanes], into, at_z(steps)))
            else:
                after.append(send(row_sum.at[which, k, up(y, steps), :, lanes], into, at_y(steps)))
        return after

    def row_scatters2(which, k, copies):
        return row_scatter2(which, k, 0, copies[0]) + row_scatter2(which, k, 1, copies[1])

    def row_total(which, k, half):
        lanes = halves[half]
        total = row_sum[which, k, y if half else z, :, lanes].astype(F32)
        for index in range(3):
            total = total + row_in2[which, k, index, :, lanes].astype(F32)
        return total

    def mm_out(k, pairs):
        arrive(pairs)
        product = nn_dot(act[k, :, 0:UNITS], wd[...]).astype(BF16)
        row_part[0, k] = product.reshape(4, 4, SUB, FEATS)
        return row_scatter1(0, k, 0), row_scatter1(0, k, 1)

    def mm_in_back(k, pairs, pieces=1):
        arrive(pairs)
        keep(act.at[k, :, pl.ds(2 * UNITS, UNITS)], d_up_all.at[k])
        copies = ([], [])
        width = HALF // pieces
        for piece in range(pieces):
            for half in range(2):
                lanes = slice(half * HALF + piece * width, half * HALF + (piece + 1) * width)
                product = nt_dot(act[k, :, UNITS : 2 * UNITS], wg[lanes, :]) + nt_dot(
                    act[k, :, 2 * UNITS : 3 * UNITS], wu[lanes, :]
                )
                row_part[1, k, :, :, :, lanes] = product.astype(BF16).reshape(4, 4, SUB, width)
                copies[half].extend(row_scatter1(1, k, half, piece * width, width))
        return copies

    def finish_out(k, copies):
        arrive(copies)
        rows = slice(k * SUB, (k + 1) * SUB)
        for half, lanes in enumerate(halves):
            output[rows, lanes] = (inputs[rows, lanes].astype(F32) + row_total(0, k, half)).astype(BF16)

    def finish_in(k, copies):
        arrive(copies)
        rows = slice(k * SUB, (k + 1) * SUB)
        for half, lanes in enumerate(halves):
            d_norm[rows, lanes] = row_total(1, k, half)

    def early_grad(left_of, right, early, first, last):
        def body(m, carry):
            at = pl.multiple_of(m * TILE, TILE)
            early[m] = tn_dot(left_of(0, 2, at), right(0, 2)).astype(BF16)
            return carry

        lax.fori_loop(first, last, body, 0)

    def weight_grad(left_of, right, early, wide_mask, target, stage, sems, first, last, reuse):
        def body(m, carry):
            at = pl.multiple_of(m * TILE, TILE)
            use = lax.rem(m, 2)

            def store():
                return pltpu.make_async_copy(stage.at[use], target.at[pl.ds(at, TILE), :], sems.at[use])

            if reuse:
                store().wait()
            else:
                @pl.when(m >= 2)
                def _():
                    store().wait()

            product = tn_dot(left_of(2, 3, at), right(2, 3)) + early[m].astype(F32)
            stage[use] = masked(product, wide_mask[pl.ds(m * 4, 4)])
            store().start()
            return carry

        lax.fori_loop(first, last, body, 0)

    def act_of(start, width):
        def get(k0, k1):
            return act[k0:k1, :, start : start + width].reshape((k1 - k0) * 256, width)

        return get

    def act_left(k0, k1, at):
        return act[k0:k1, :, pl.ds(at, TILE)].reshape((k1 - k0) * 256, TILE)

    def cot_right(k0, k1):
        return cot[k0:k1].reshape((k1 - k0) * 256, FEATS)

    def hid_left(k0, k1, at):
        return hid[k0:k1, :, :, :, pl.ds(at, TILE)].reshape((k1 - k0) * 256, TILE)

    d_gate_right = act_of(UNITS, UNITS)

    def early_down(first, last):
        early_grad(act_left, cot_right, down_early, first, last)

    def early_gate(first, last):
        early_grad(hid_left, d_gate_right, gate_early, first, last)

    def grad_down(first, last, reuse):
        weight_grad(
            act_left, cot_right, down_early, ed, grad_w_down, stage_d, store_sem.at[0], first, last, reuse
        )

    def grad_gate(first, last, reuse):
        weight_grad(
            hid_left, d_gate_right, gate_early, eg, grad_w_gate, stage_u, store_sem.at[1], first, last, reuse
        )

    all_job, out_job, in_job = (0, 3 * UNITS), (0, UNITS), (UNITS, 2 * UNITS)
    pd0 = mm_down_back(0)
    hid1.append(gather1(hid, 1))
    arrive(cot1[1])
    cot2.append(gather2(cot, 1))
    mask_weights(wg, eg, loads[1])
    sd0 = scatter1(0, down_job, pd0)
    cot1.append(gather1(cot, 2))
    hid1.append(gather1(hid, 2))
    mask_weights(wu, eu, loads[2])
    pg0 = mm_gate(0)
    pu0 = mm_up(0)
    arrive(hid1[1])
    hid2.append(gather2(hid, 1))
    sg0 = scatter1(0, gate_job, pg0)
    td0 = scatter2(0, down_job, sd0)
    su0 = scatter1(0, up_job, pu0)
    arrive(cot1[2])
    cot2.append(gather2(cot, 2))
    arrive(hid1[2])
    hid2.append(gather2(hid, 2))
    pd1 = mm_down_back(1)
    tg0 = scatter2(0, gate_job, sg0)
    pg1 = mm_gate(1) + mm_up(1)
    tu0 = scatter2(0, up_job, su0)
    sd1 = scatter1(1, down_job, pd1)
    sg1 = scatter1(1, gate_up_job, pg1)
    pd2 = mm_down_back(2)
    pg2 = mm_gate(2) + mm_up(2)
    for k in range(CHUNKS):
        keep(hid.at[k], hid_all.at[k])
    td1 = scatter2(1, down_job, sd1)
    activate(0, td0 + tg0 + tu0)
    a0 = spread1(0, all_job)
    sd2 = scatter1(2, down_job, pd2)
    tg1 = scatter2(1, gate_up_job, sg1)
    sg2 = scatter1(2, gate_up_job, pg2)
    h0, q0 = spread2(0, all_job, a0)
    activate(1, td1 + tg1)
    a1 = spread1(1, all_job)
    td2 = scatter2(2, down_job, sd2)
    r0 = spread3(0, all_job, h0, q0)
    tg2 = scatter2(2, gate_up_job, sg2)
    n0 = mm_in_back(0, r0)
    h1, q1 = spread2(1, all_job, a1)
    activate(2, td2 + tg2)
    a2 = spread1(2, in_job)
    b2 = spread1(2, out_job)
    o0 = mm_out(0, ())
    r1 = spread3(1, all_job, h1, q1)
    n0 = row_scatters2(1, 0, n0)
    o0 = row_scatters2(0, 0, o0)
    n1 = mm_in_back(1, r1)
    h2, q2 = spread2(2, in_job, a2)
    o1 = mm_out(1, ())
    early_gate(0, 2)
    u2, v2 = spread2(2, out_job, b2)
    early_gate(2, 4)
    r2 = spread3(2, in_job, h2, q2)
    n1 = row_scatters2(1, 1, n1)
    w2 = spread3(2, out_job, u2, v2)
    early_down(0, 3)
    n2 = mm_in_back(2, r2, 2)
    o2 = mm_out(2, w2)
    o1 = row_scatters2(0, 1, o1)
    finish_out(0, o0)
    finish_in(0, n0)
    finish_in(1, n1)
    early_down(3, 7)
    n2 = row_scatters2(1, 2, n2)
    grad_gate(0, 2, False)
    o2 = row_scatters2(0, 2, o2)
    grad_gate(2, 4, True)
    finish_out(1, o1)
    grad_down(0, 2, False)
    finish_in(2, n2)

    moved = d_norm[...] * normed[...]
    in_own[...] = lane_fold(moved * gain[...])
    inner = all_col(in_own, in_in)
    gn_own[...] = jnp.sum(moved, axis=0, keepdims=True)
    gains = [send(gn_own, gn_in.at[index], device) for index, device in enumerate(row_peers)]
    finish_out(2, o2)
    keep(output, output_at)
    grad_down(2, 7, True)
    arrive(inner)
    inner_all = in_own[...]
    for index in range(7):
        inner_all = inner_all + in_in[index]
    row_inner = jnp.sum(inner_all, axis=1, keepdims=True) / D
    grad_inputs[...] = (
        grad_out[...].astype(F32)
        + inv_rms[:, 0:1] * (d_norm[...] * gain[...] - normed[...] * row_inner)
    ).astype(BF16)
    keep(grad_inputs, grad_inputs_at)
    arrive(gains)
    gain_total = gn_own[...]
    for index in range(15):
        gain_total = gain_total + gn_in[index]
    grad_gain[...] = gain_total
    keep(grad_gain, grad_gain_at)
    for use in range(2):
        pltpu.make_async_copy(stage_d.at[use], grad_w_down.at[pl.ds(0, TILE), :], store_sem.at[0, use]).wait()
        pltpu.make_async_copy(stage_u.at[use], grad_w_gate.at[pl.ds(0, TILE), :], store_sem.at[1, use]).wait()
    for copy in kept:
        copy.wait()
    for copy in started:
        copy.wait_send()


def last_grad(
    output_in, grad_inputs_in, grad_gain_in, grad_w_gate_in, grad_w_down_in, d_up_all, hid_all, mask_up,
    output, grad_inputs, grad_gain, grad_w_gate, grad_w_up, grad_w_down,
    d_up, hid, eu, small_a, small_b, small_c, big_a, big_b, stage, need_sem, in_sem, out_sem,
):
    needs = [
        pltpu.make_async_copy(d_up_all, d_up, need_sem.at[0]),
        pltpu.make_async_copy(hid_all, hid, need_sem.at[1]),
    ]
    for need in needs:
        need.start()
    moves = [
        (output_in, small_a, output, slice(0, LOCAL)),
        (grad_inputs_in, small_b, grad_inputs, slice(0, LOCAL)),
        (grad_gain_in, small_c, grad_gain, slice(0, 1)),
    ]
    for source, held, target in ((grad_w_gate_in, big_a, grad_w_gate), (grad_w_down_in, big_b, grad_w_down)):
        rows = source.shape[0] // 4
        moves += [(source, held, target, slice(n * rows, (n + 1) * rows)) for n in range(4)]
    loads = [
        pltpu.make_async_copy(source.at[rows, :], held.at[rows, :], in_sem.at[index])
        for index, (source, held, target, rows) in enumerate(moves)
    ]
    saves = []

    def move(count):
        for _ in range(count):
            index = len(saves)
            source, held, target, rows = moves[index]
            loads[index].wait()
            saves.append(pltpu.make_async_copy(held.at[rows, :], target.at[rows, :], out_sem.at[index]))
            saves[-1].start()

    widen(mask_up[...], eu)
    for need in needs:
        need.wait()
    for load in loads:
        load.start()
    grads = []
    tokens = CHUNKS * 256
    for m in range(FEATS // TILE):
        rows = slice(m * TILE, (m + 1) * TILE)
        product = tn_dot(
            hid[:, :, :, :, rows].reshape(tokens, TILE), d_up[...].reshape(tokens, UNITS)
        )
        stage[m] = masked(product, eu[m * 4 : (m + 1) * 4])
        grads.append(pltpu.make_async_copy(stage.at[m], grad_w_up.at[rows, :], need_sem.at[m + 2]))
        grads[-1].start()
        move((2, 3, 3, 3)[m])
    for copy in saves + grads:
        copy.wait()


def shards(inputs, norm_gain, w_gate, w_up, w_down, mask_gate, mask_up, mask_down, grad_out):
    vmem = pl.BlockSpec(memory_space=pltpu.VMEM)
    anywhere = pl.BlockSpec(memory_space=pl.ANY)
    wide = 3 * UNITS
    shape = jax.ShapeDtypeStruct
    results = pl.pallas_call(
        layer,
        out_shape=(
            shape((LOCAL, FEATS), BF16),
            shape((LOCAL, FEATS), BF16),
            shape((1, FEATS), F32),
            shape((FEATS, UNITS), BF16),
            shape((UNITS, FEATS), BF16),
            shape((CHUNKS, 256, UNITS), BF16),
            shape((CHUNKS, 4, 4, SUB, FEATS), BF16),
        ),
        in_specs=[anywhere] * 9,
        out_specs=(anywhere,) * 7,
        scratch_shapes=[
            pltpu.VMEM((LOCAL, FEATS), BF16),
            pltpu.VMEM((1, FEATS), F32),
            pltpu.VMEM((FEATS // BLOCK, UNITS // BLOCK), jnp.int32),
            pltpu.VMEM((FEATS // BLOCK, UNITS // BLOCK), jnp.int32),
            pltpu.VMEM((FEATS // BLOCK, UNITS // BLOCK), jnp.int32),
            pltpu.VMEM((LOCAL, FEATS), BF16),
            pltpu.VMEM((LOCAL, FEATS), BF16),
            pltpu.VMEM((LOCAL, FEATS), BF16),
            pltpu.VMEM((1, FEATS), F32),
            pltpu.VMEM((FEATS // TILE, TILE, UNITS), BF16),
            pltpu.VMEM((UNITS // TILE, TILE, FEATS), BF16),
            pltpu.VMEM((FEATS, UNITS), BF16),
            pltpu.VMEM((FEATS, UNITS), BF16),
            pltpu.VMEM((UNITS, FEATS), BF16),
            pltpu.VMEM((FEATS // BLOCK, SUB, UNITS), BF16),
            pltpu.VMEM((FEATS // BLOCK, SUB, UNITS), BF16),
            pltpu.VMEM((UNITS // BLOCK, SUB, FEATS), BF16),
            pltpu.VMEM((CHUNKS, 4, 4, SUB, FEATS), BF16),
            pltpu.VMEM((CHUNKS, 4, 4, SUB, FEATS), BF16),
            pltpu.VMEM((CHUNKS, 256, wide), BF16),
            pltpu.VMEM((CHUNKS, 128, wide), BF16),
            pltpu.VMEM((CHUNKS, SUB, wide), BF16),
            pltpu.VMEM((CHUNKS, SUB, wide), BF16),
            pltpu.VMEM((CHUNKS, 32, wide), BF16),
            pltpu.VMEM((CHUNKS, 32, wide), BF16),
            pltpu.VMEM((CHUNKS, 256, wide), BF16),
            pltpu.VMEM((2, CHUNKS, 4, 4, SUB, FEATS), BF16),
            pltpu.VMEM((2, CHUNKS, 3, 4, SUB, FEATS), BF16),
            pltpu.VMEM((2, CHUNKS, 4, SUB, FEATS), BF16),
            pltpu.VMEM((2, CHUNKS, 3, SUB, FEATS), BF16),
            pltpu.VMEM((LOCAL, FEATS), F32),
            pltpu.VMEM((LOCAL, 128), F32),
            pltpu.VMEM((LOCAL, FEATS), F32),
            pltpu.VMEM((LOCAL, 128), F32),
            pltpu.VMEM((7, LOCAL, 128), F32),
            pltpu.VMEM((LOCAL, 128), F32),
            pltpu.VMEM((7, LOCAL, 128), F32),
            pltpu.VMEM((1, FEATS), F32),
            pltpu.VMEM((15, 1, FEATS), F32),
            pltpu.VMEM((2, TILE, FEATS), BF16),
            pltpu.VMEM((2, TILE, UNITS), BF16),
            pltpu.SemaphoreType.DMA((COPIES,)),
            pltpu.SemaphoreType.DMA((COPIES,)),
            pltpu.SemaphoreType.DMA((3,)),
            pltpu.SemaphoreType.DMA((2, 2)),
            pltpu.SemaphoreType.DMA((2 * CHUNKS + 3,)),
            pltpu.SemaphoreType.DMA((6,)),
        ],
        compiler_params=pltpu.CompilerParams(
            collective_id=0, has_side_effects=True, vmem_limit_bytes=60 << 20
        ),
        name="layer",
    )(
        inputs, norm_gain.reshape(1, FEATS), w_gate, w_up, w_down,
        mask_gate, mask_up, mask_down.T, grad_out,
    )
    output, grad_inputs, grad_gain, grad_w_gate, grad_w_up, grad_w_down = pl.pallas_call(
        last_grad,
        out_shape=(
            shape((LOCAL, FEATS), BF16),
            shape((LOCAL, FEATS), BF16),
            shape((1, FEATS), F32),
            shape((FEATS, UNITS), BF16),
            shape((FEATS, UNITS), BF16),
            shape((UNITS, FEATS), BF16),
        ),
        in_specs=[anywhere] * 7 + [vmem],
        out_specs=(anywhere,) * 6,
        scratch_shapes=[
            pltpu.VMEM((CHUNKS, 256, UNITS), BF16),
            pltpu.VMEM((CHUNKS, 4, 4, SUB, FEATS), BF16),
            pltpu.VMEM((FEATS // BLOCK, SUB, UNITS), BF16),
            pltpu.VMEM((LOCAL, FEATS), BF16),
            pltpu.VMEM((LOCAL, FEATS), BF16),
            pltpu.VMEM((1, FEATS), F32),
            pltpu.VMEM((FEATS, UNITS), BF16),
            pltpu.VMEM((UNITS, FEATS), BF16),
            pltpu.VMEM((4, TILE, UNITS), BF16),
            pltpu.SemaphoreType.DMA((6,)),
            pltpu.SemaphoreType.DMA((11,)),
            pltpu.SemaphoreType.DMA((11,)),
        ],
        compiler_params=pltpu.CompilerParams(vmem_limit_bytes=60 << 20),
        name="last_grad",
    )(*results, mask_up)
    return output, grad_inputs, grad_gain.reshape(FEATS), grad_w_gate, grad_w_up, grad_w_down


def solution(mesh):
    in_specs = (
        P("row", "col"),
        P("col"),
        P("col", "row"),
        P("col", "row"),
        P("row", "col"),
        P("col", "row"),
        P("col", "row"),
        P("row", "col"),
        P("row", "col"),
    )
    out_specs = (
        P("row", "col"),
        P("row", "col"),
        P("col"),
        P("col", "row"),
        P("col", "row"),
        P("row", "col"),
    )
    return jax.shard_map(shards, mesh=mesh, in_specs=in_specs, out_specs=out_specs, check_vma=False)
```
